32 devices in a mesh: seq: 8 (over z, x), head: 4 (over y, core).
Axes of the slice: x: 2, y: 2, z: 4, core: 2. Of those that a mesh axis runs over, the one named last changes fastest.
Arguments:
- tokens: bfloat16 [8192, 768], P('seq'), may hold values from -6 to 6
- slide_ids: int32 [8192], P('seq'), may hold values from 0 to 3, never falling along the last dimension, each value on 1 to 4096 neighbouring positions
- valid: int32 [8192], P('seq'), may hold values 0 or 1
- norm_one: float32 [768], replicated, may hold values from 0.1 to 1.9
- w_qkv: bfloat16 [3, 768, 768], P(None, None, 'head'), may hold values from -0.21875 to 0.21875
- w_out: bfloat16 [768, 768], P('head'), may hold values from -2.5 to 2.5
- norm_two: float32 [768], replicated, may hold values from 0.1 to 1.9
- w_up: bfloat16 [768, 3072], P(None, 'head'), may hold values from -0.21875 to 0.21875
- w_down: bfloat16 [3072, 768], P('head'), may hold values from -0.109375 to 0.109375
- cotangent: bfloat16 [8192, 768], P('seq'), may hold values from -6 to 6
Outputs:
- output: bfloat16 [8192, 768], P('seq')
- input_grad: float32 [8192, 768], P('seq')
- grad_norm_one: float32 [768], replicated
- grad_qkv: float32 [3, 768, 768], P(None, None, 'head')
- grad_out: float32 [768, 768], P('head')
- grad_norm_two: float32 [768], replicated
- grad_up: float32 [768, 3072], P(None, 'head')
- grad_down: float32 [3072, 768], P('head')
The draws below stay inside these ranges and needn't reach their ends.
Inputs may be any that keep to these rules, and one draw needn't show every extreme that they name: `slide_ids`: slide numbers never fall along the positions; each slide has 1 to 4096 positions, one exactly 4096.
All inputs are finite; a program needn't handle non-finite values. No bound on the sum of `valid` on one device may be relied on, other than what follows from the above.
Results may differ from the reference program's by a relative error of at most 0.019.
Values may be sent and summed in bfloat16 or wider, within the bound.
A program may use at most 192 MiB of HBM per device.

```python
import math
import jax
import jax.numpy as jnp
import numpy as np
from jax import lax

D = 768
H = 16
HD = 48
FF = 3072
TOKENS = 8192
SLIDES = 4
SLIDE_MOST = 4096


def with_ends(drawn, key, low, high):
    index_at = [jax.random.randint(jax.random.fold_in(key, axis), (), 0, length) for axis, length in enumerate(drawn.shape)]
    main_axis = drawn.shape.index(max(drawn.shape))
    neighbour = index_at[:main_axis] + [(index_at[main_axis] + 1) % drawn.shape[main_axis]] + index_at[main_axis + 1:]
    return drawn.at[tuple(index_at)].set(low).at[tuple(neighbour)].set(high)


def levels(rng, dims, pieces, low, high):
    level, own = 1.0, jax.random.fold_in(rng, 6)
    for position, blocks in pieces:
        heights = jnp.exp(jax.random.uniform(jax.random.fold_in(own, position), (blocks,), jnp.float32, low / len(pieces), high / len(pieces)))
        level = level * jnp.repeat(heights, dims[position] // blocks).reshape([-1 if axis == position else 1 for axis in range(len(dims))])
    return level


def profile(number_of, total, limit, skew):
    loads = [(1 << 20) // math.isqrt(standing ** skew) + 1 for standing in range(2, number_of + 1)]
    surplus, counts = total - limit - (number_of - 1), [1] * (number_of - 1)
    while surplus > 0:
        movable = [i for i in range(number_of - 1) if counts[i] < limit]
        whole, budget = sum([loads[i] for i in movable]), surplus
        for i in movable:
            more = min(limit - counts[i], max(1, budget * loads[i] // whole), surplus)
            counts[i] = counts[i] + more
            surplus = surplus - more
    return np.array([limit] + counts)


def ragged_sizes(stream_key, count, total, most, lean):
    if count == 2:
        one = jax.random.randint(stream_key, (), max(1, total - most), min(most, total - 1) + 1)
        return jnp.stack([one, total - one])
    lengths = jnp.asarray(profile(count, total, most, lean), jnp.int32)
    twos = (count - 1) // 2
    giver, sink = lengths[1:1 + 2 * twos:2], lengths[2:2 + 2 * twos:2]
    room = jnp.minimum(giver - 1, most - sink)
    moved = jax.random.randint(jax.random.fold_in(stream_key, 1), (twos,), 0, 1 << 20) % (room + 1)
    lengths = lengths.at[1:1 + 2 * twos:2].set(giver - moved).at[2:2 + 2 * twos:2].set(sink + moved)
    return lengths[jax.random.permutation(jax.random.fold_in(stream_key, 2), count)]


def noise(own_key, extent, scale, most, pieces=(), held_as=jnp.bfloat16):
    values = jax.random.normal(own_key, extent, jnp.float32) * scale
    if len(pieces) > 0:
        values = levels(own_key, extent, pieces, -0.22, 0.18) * values
    return jnp.clip(values, min=-most, max=most).astype(held_as)


def setup_inputs(seed: int = 0) -> dict:
    keys = jax.random.split(jax.random.key(seed), 11)
    tokens = noise(keys[0], (TOKENS, D), 1.0, 6.0, ((0, 8),))
    slide_ids = jnp.searchsorted(jnp.cumsum(ragged_sizes(keys[1], SLIDES, TOKENS, SLIDE_MOST, 2)), jnp.arange(TOKENS), side="right").astype(jnp.int32)
    valid = with_ends((jax.random.randint(keys[2], (TOKENS,), 0, 8) < 7).astype(jnp.int32), jax.random.fold_in(keys[2], 1), 0, 1)
    norm_one = jnp.clip(1.0 + 0.18 * jax.random.normal(keys[3], (D,), jnp.float32), 0.1, 1.9)
    w_qkv = noise(keys[4], (3, D, D), D ** -0.5, 0.21875, ((2, 4),))
    w_out = noise(keys[5], (D, D), (D // 128) ** -0.5, 2.5, ((0, 4),))
    norm_two = jnp.clip(1.0 + 0.18 * jax.random.normal(keys[6], (D,), jnp.float32), 0.1, 1.9)
    w_up = noise(keys[7], (D, FF), D ** -0.5, 0.21875, ((1, 4),))
    w_down = noise(keys[8], (FF, D), FF ** -0.5, 0.109375, ((0, 4),))
    cotangent = noise(keys[9], (TOKENS, D), 1.0, 6.0, ((0, 8),))
    return dict(tokens=tokens, slide_ids=slide_ids, valid=valid, norm_one=norm_one, w_qkv=w_qkv, w_out=w_out, norm_two=norm_two, w_up=w_up, w_down=w_down, cotangent=cotangent)


seg_lengths = (1024, 2048, 4096, 8192, 16384)
ratios = (1, 2, 4, 8, 16)
eps = 1e-05
masked = -1e+30

@jax.custom_vjp
def low(v):
    return lax.optimization_barrier(v.astype(jnp.bfloat16)).astype(jnp.float32)

@jax.custom_vjp
def low_back(v):
    return v

def low_keep(v):
    return (low(v), None)

def low_pass(kept, grad):
    return (grad,)

def back_keep(v):
    return (v, None)

def back_low(kept, grad):
    return (low(grad),)
low.defvjp(low_keep, low_pass)
low_back.defvjp(back_keep, back_low)

def product(left, right):
    return jnp.dot(left, right, precision=lax.Precision.HIGHEST, preferred_element_type=jnp.float32)

def normalize(rows_in, gain):
    centre = rows_in - lax.optimization_barrier(jnp.mean(rows_in, axis=-1, keepdims=True))
    spread = lax.optimization_barrier(jnp.mean(centre * centre, axis=-1, keepdims=True))
    return centre * lax.rsqrt(spread + eps) * gain

def branch(query, keyset, valueset, tags, seg, rate):
    segments = TOKENS // seg
    per_segment = seg // rate
    offsets = jnp.arange(H, dtype=jnp.int32) % rate
    chosen = jnp.arange(rate, dtype=jnp.int32)[:, None] == offsets[None, :]

    def pick(array):
        shaped = array.reshape(segments, per_segment, rate, H, HD)
        return lax.optimization_barrier(jnp.sum(jnp.where(chosen[None, None, :, :, None], shaped, 0.0), axis=2))
    shaped_tags = jnp.broadcast_to(tags.reshape(segments, per_segment, rate, 1), (segments, per_segment, rate, H))
    picked_tags = lax.optimization_barrier(jnp.sum(jnp.where(chosen[None, None], shaped_tags, 0), axis=2, dtype=jnp.int32))
    factor = HD ** (-0.5)

    def segment(parts):
        queries, key_rows, value_rows, labels = parts
        raw = jnp.einsum('qhd,khd->hqk', queries, key_rows, precision=lax.Precision.HIGHEST) * factor
        raw = low_back(raw)
        query_tag = labels.T[:, :, None]
        key_tag = labels.T[:, None, :]
        allowed = (query_tag // 2 == key_tag // 2) & ((key_tag % 2 == 1) | (query_tag % 2 == 0))
        scores = jnp.where(allowed, raw, masked)
        highest = lax.optimization_barrier(jnp.max(scores, axis=-1, keepdims=True))
        log_total = highest + jnp.log(lax.optimization_barrier(jnp.sum(jnp.exp(scores - highest), axis=-1, keepdims=True)))
        weights = low(jnp.exp(scores - log_total))
        result = jnp.einsum('hqk,khd->qhd', weights, value_rows, precision=lax.Precision.HIGHEST)
        return (result, log_total[:, :, 0].T)
    outs, totals = lax.map(jax.checkpoint(segment), (pick(query), pick(keyset), pick(valueset), picked_tags))
    full_out = jnp.where(chosen[None, None, :, :, None], outs[:, :, None], 0.0).reshape(TOKENS, H, HD)
    full_total = jnp.where(chosen[None, None], totals[:, :, None], masked).reshape(TOKENS, H)
    return (full_out, full_total)

def forward(inputs, gain_one, w_qkv, w_out, gain_two, w_up, w_down, tags):
    normed = low(normalize(inputs, gain_one))
    mixed = jnp.einsum('td,cde->cte', normed, w_qkv, precision=lax.Precision.HIGHEST)
    mixed = low(low_back(mixed))
    query = mixed[0].reshape(TOKENS, H, HD)
    keyset = mixed[1].reshape(TOKENS, H, HD)
    valueset = mixed[2].reshape(TOKENS, H, HD)
    parts, totals = ([], [])
    for seg, rate in zip(seg_lengths, ratios):
        result, log_total = branch(query, keyset, valueset, tags, min(seg, TOKENS), rate)
        parts.append(result)
        totals.append(log_total)
    stacked = jnp.stack(totals)
    highest = lax.optimization_barrier(jnp.max(stacked, axis=0))
    bound = highest + jnp.log(lax.optimization_barrier(jnp.sum(jnp.exp(stacked - highest[None]), axis=0)))
    attn = parts[0] * jnp.exp(totals[0] - bound)[:, :, None]
    for which in range(1, len(parts)):
        attn = attn + parts[which] * jnp.exp(totals[which] - bound)[:, :, None]
    attn = low(low_back(attn.reshape(TOKENS, D)))
    middle = inputs + low_back(product(attn, w_out))
    second = low(normalize(middle, gain_two))
    hidden = low(jax.nn.gelu(low_back(product(second, w_up)), approximate=False))
    return middle + product(hidden, w_down)

def reference(tokens, slide_ids, valid, norm_one, w_qkv, w_out, norm_two, w_up, w_down, cotangent):
    tags = 2 * slide_ids + valid
    arrays = (tokens.astype(jnp.float32), norm_one, w_qkv.astype(jnp.float32), w_out.astype(jnp.float32), norm_two, w_up.astype(jnp.float32), w_down.astype(jnp.float32))

    def closed(inputs, gain_one, proj_qkv, proj_out, gain_two, proj_up, proj_down):
        return forward(inputs, gain_one, proj_qkv, proj_out, gain_two, proj_up, proj_down, tags)
    result, pull = jax.vjp(closed, *arrays)
    grads = pull(cotangent.astype(jnp.float32))
    return (result.astype(jnp.bfloat16), grads[0], grads[1], grads[2], grads[3], grads[4], grads[5], grads[6])
```

```python
from functools import partial

import jax
import jax.numpy as jnp
from jax import lax
from jax.experimental import pallas as pl
from jax.experimental.pallas import tpu as pltpu
from jax.sharding import PartitionSpec as P

HD = 48
SLOT = 64
CLASSES = 16
CHUNK = CLASSES * 16
EPS = 1e-05
NEG = -(2.0**30)
LOG2E = 1.4426950408889634
FACTOR = HD ** (-0.5)
MESH = pl.DeviceIdType.MESH
f32 = jnp.float32
bf16 = jnp.bfloat16
NT = (((1,), (1,)), ((), ()))
VMEM = pl.BlockSpec(memory_space=pltpu.VMEM)
LIMIT = 60 * 1024 * 1024


def dot(a, b):
    return jnp.dot(a, b, preferred_element_type=f32)


def dot_nt(a, b):
    return lax.dot_general(a, b, NT, preferred_element_type=f32)


def iota(shape, dim):
    return lax.broadcasted_iota(jnp.int32, shape, dim)


def one_hot(cond):
    return jnp.where(cond, 1.0, 0.0).astype(bf16)


def digit_swap():
    row, col = iota((CHUNK, CHUNK), 0), iota((CHUNK, CHUNK), 1)
    return one_hot(col == 16 * (row % 16) + row // 16)


def spreader(width):
    row, col = iota((width, width // HD * SLOT), 0), iota((width, width // HD * SLOT), 1)
    return one_hot(col == SLOT * (row // HD) + row % HD)


def unspreader(width):
    row, col = iota((width // HD * SLOT, width), 0), iota((width // HD * SLOT, width), 1)
    return one_hot(row == SLOT * (col // HD) + col % HD)


def eye(size):
    return one_hot(iota((size, size), 0) == iota((size, size), 1))


def bit_reverse(i):
    return i % 2 * 8 + i // 2 % 2 * 4 + i // 4 % 2 * 2 + i // 8


def peer_of(me, apart):
    out = me
    for bit in range(apart.bit_length()):
        if apart >> bit & 1:
            out = out + (1 << bit) * (1 - 2 * (me // (1 << bit) % 2))
    return out


def level_count(n_seq):
    count = 0
    while count < 4 and 2 << count <= n_seq:
        count += 1
    return count


def slots_of(level, half):
    rows = half >> level
    return [
        (apart, level * half + (apart - (1 << level)) * rows, rows)
        for apart in range(1 << level, 2 << level)
    ]


def depth_of(index, half):
    total = jnp.zeros(index.shape, f32)
    for level in range(4):
        total = total + jnp.where(index < half >> level, 1.0, 0.0)
    return total


def pair_counts(keys, queries, half, level):
    period = half if level is None else half >> level
    key = depth_of(iota((keys, queries), 0) % period, half)
    query = depth_of(iota((keys, queries), 1), half)
    return jnp.minimum(key, query) + (1.0 if level is None else -1.0 * level)


def greet(peers, axis):
    barrier = pltpu.get_barrier_semaphore()
    for peer in peers:
        pl.semaphore_signal(barrier, inc=1, device_id={axis: peer}, device_id_type=MESH)
    pl.semaphore_wait(barrier, len(peers))


def half_mask(which, rows):
    lane = iota((rows, 2 * SLOT), 1)
    return one_hot(lane // SLOT == which)


def to_classes(value, t, cls_ref, lanes, block):
    for c in range(CLASSES):
        start = pl.multiple_of(c * block + t * 16, 16)
        cls_ref[pl.ds(start, 16), lanes] = value[16 * c : 16 * c + 16]


def class_start(i, head, block):
    return pl.multiple_of((bit_reverse(i) + head) % CLASSES * block, block)


def place_start(c, head, block):
    return pl.multiple_of(bit_reverse((c + CLASSES - head) % CLASSES) * block, block)


def from_heads(src_refs, base, dst_ref, block):
    low = iota((block, 2 * SLOT), 1) < SLOT

    def step(c, carry):
        for tile, (ref, pair) in enumerate(src_refs):
            left = ref[pair, pl.ds(place_start(c, base + 2 * pair, block), block), :]
            right = ref[pair, pl.ds(place_start(c, base + 2 * pair + 1, block), block), :]
            both = jnp.where(low, left, right).astype(bf16)
            for t in range(block // 16):
                start = pl.multiple_of(t * CHUNK + c * 16, 16)
                dst_ref[pl.ds(start, 16), tile * 128 : tile * 128 + 128] = both[16 * t : 16 * t + 16]
        return carry

    lax.fori_loop(0, CLASSES, step, 0)


def project_kernel(heads, tokens_ref, aux_ref, gain_ref, w_ref, normed_ref, qz_ref, kv_ref, cls_ref):
    rows = tokens_ref.shape[0]
    block = rows // CLASSES
    width = heads * HD
    wide = heads * SLOT
    swap = digit_swap()
    spread = spreader(width)
    ones = jnp.where(iota((CHUNK, wide), 1) % SLOT >= HD, 1.0, 0.0)

    def step(t, carry):
        here = pl.ds(pl.multiple_of(t * CHUNK, CHUNK), CHUNK)
        x = tokens_ref[here, :].astype(f32)
        centre = x - jnp.mean(x, axis=-1, keepdims=True)
        spread_of = jnp.mean(centre * centre, axis=-1, keepdims=True)
        normed = (centre * lax.rsqrt(spread_of + EPS) * gain_ref[...]).astype(bf16)
        normed_ref[here, :] = normed
        for c in range(3):
            y = dot(normed, w_ref[c])
            if c == 1:
                y = y * (FACTOR * LOG2E)
            y = dot(y.astype(bf16), spread)
            if c < 2:
                y = y + aux_ref[here, c * wide : c * wide + wide].astype(f32)
            else:
                y = y + ones
            y = dot(swap, y.astype(bf16)).astype(bf16)
            to_classes(y, t, cls_ref, slice(c * wide, c * wide + wide), block)
        return carry

    lax.fori_loop(0, rows // CHUNK, step, 0)
    base = lax.axis_index("head") * heads
    masks = [half_mask(0, block), half_mask(1, block)]

    def pick(i, carry):
        out = pl.ds(pl.multiple_of(i * block, block), block)
        for j in range(heads):
            src = pl.ds(class_start(i, base + j, block), block)
            lanes = slice(j // 2 * 128, j // 2 * 128 + 128)
            qz_ref[j, out, :] = cls_ref[src, lanes] * masks[j % 2]
        for tile in range(heads):
            pair = tile % (heads // 2)
            lanes = slice(wide + tile * 128, wide + tile * 128 + 128)
            left = cls_ref[pl.ds(class_start(i, base + 2 * pair, block), block), lanes]
            right = cls_ref[pl.ds(class_start(i, base + 2 * pair + 1, block), block), lanes]
            kv_ref[tile, out, :] = left * masks[0] + right * masks[1]
        return carry

    lax.fori_loop(0, CLASSES, pick, 0)


def transpose_heads(ref, first, start, count, out_ref, heads):
    unit = eye(2 * SLOT)
    for pair in range(heads // 2):
        turned = dot_nt(unit, ref[first + pair, start : start + count, :]).astype(bf16)
        out_ref[2 * pair, :, :count] = turned[:SLOT]
        out_ref[2 * pair + 1, :, :count] = turned[SLOT:]


def attend_kernel(
    levels, heads, qz_ref, kv_ref, attn_ref, attn_t_ref, bound_ref, rk_ref,
    vt_ref, s_ref, p_ref, acc_ref, m_ref, a_ref, d_ref, send_sem, recv_sem,
):
    rows = kv_ref.shape[1]
    half = rows // 2
    block = rows // CLASSES
    me = lax.axis_index("seq")
    slots = [slot for level in range(levels) for slot in slots_of(level, half)]
    greet([peer_of(me, apart) for apart, _, _ in slots], "seq")
    copies = {}
    for apart, offset, count in slots:
        copies[apart] = pltpu.make_async_remote_copy(
            src_ref=kv_ref.at[:, 0:count, :],
            dst_ref=rk_ref.at[:, offset : offset + count, :],
            send_sem=send_sem.at[apart - 1],
            recv_sem=recv_sem.at[apart - 1],
            device_id={"seq": peer_of(me, apart)},
            device_id_type=MESH,
        )
        copies[apart].start()
    transpose_heads(kv_ref, heads // 2, 0, rows, vt_ref, heads)

    def local(pair, carry):
        counts = pair_counts(half, half, half, None)
        for qt in range(2):
            there = slice(qt * half, qt * half + half)
            for side in range(2):
                h = 2 * pair + side
                s_ref[side] = dot_nt(kv_ref[pair], qz_ref[h, there, :])
                top = jnp.max(s_ref[side], axis=0, keepdims=True)
                low = jnp.exp2(s_ref[side, :half] - top)
                if qt == 0:
                    low = low * counts
                p_ref[side, :half] = low.astype(bf16)
                p_ref[side, half:] = jnp.exp2(s_ref[side, half:] - top).astype(bf16)
                acc_ref[h, :, there] = dot(vt_ref[h], p_ref[side])
                m_ref[h, :, there] = top
        return carry

    lax.fori_loop(0, heads // 2, local, 0)

    for level in range(levels):
        queries = max(half >> level, 128)
        for apart, _, _ in slots_of(level, half):
            copies[apart].wait_recv()
        keys = slice(level * half, level * half + half)
        transpose_heads(rk_ref, heads // 2, level * half, half, vt_ref, heads)

        def remote(pair, carry):
            counts = pair_counts(half, queries, half, level)
            for side in range(2):
                h = 2 * pair + side
                s = dot_nt(rk_ref[pair, keys, :], qz_ref[h, :queries, :])
                if half >> level < queries:
                    s = s + jnp.where(counts > 0.0, 0.0, NEG)
                old = m_ref[h, :, :queries]
                top = jnp.maximum(old, jnp.max(s, axis=0, keepdims=True))
                p = (jnp.exp2(s - top) * counts).astype(bf16)
                acc_ref[h, :, :queries] = acc_ref[h, :, :queries] * jnp.exp2(old - top) + dot(
                    vt_ref[h, :, :half], p
                )
                m_ref[h, :, :queries] = top
            return carry

        lax.fori_loop(0, heads // 2, remote, 0)

    for h in range(heads):
        total = acc_ref[h, HD : HD + 1, :]
        bound_ref[h] = m_ref[h] + jnp.log2(total)
        attn_t_ref[h] = acc_ref[h] * (1.0 / total)
    for pair in range(heads // 2):
        a_ref[pair] = jnp.concatenate([attn_t_ref[2 * pair], attn_t_ref[2 * pair + 1]], axis=0).T
    base = lax.axis_index("head") * heads
    from_heads([(a_ref, pair) for pair in range(heads // 2)], base, d_ref, block)
    swap = digit_swap()
    unspread = unspreader(heads * HD)
    for t in range(rows // CHUNK):
        here = slice(t * CHUNK, t * CHUNK + CHUNK)
        natural = dot(swap, d_ref[here, :]).astype(bf16)
        attn_ref[here, :] = dot(natural, unspread).astype(bf16)
    for apart, _, _ in slots:
        copies[apart].wait_send()


def attend_back_kernel(
    levels, heads, qz_ref, kv_ref, rk_ref, da_ref, attn_t_ref, bound_ref, dmixed_ref,
    cls_ref, doz_ref, delta_ref, kt_ref, p_ref, ds_ref, dkv_ref, dqt_ref, dq_ref, sb_ref, rg_ref, d_ref,
    send_sem, recv_sem,
):
    rows = kv_ref.shape[1]
    half = rows // 2
    block = rows // CLASSES
    pairs = heads // 2
    wide = heads * SLOT
    me = lax.axis_index("seq")
    base = lax.axis_index("head") * heads
    slots = [slot for level in range(levels) for slot in slots_of(level, half)]
    greet([peer_of(me, apart) for apart, _, _ in slots], "seq")
    swap = digit_swap()
    spread = spreader(heads * HD)
    for t in range(rows // CHUNK):
        y = dot(da_ref[t * CHUNK : t * CHUNK + CHUNK, :], spread).astype(bf16)
        y = dot(swap, y).astype(bf16)
        to_classes(y, t, cls_ref, slice(0, wide), block)
    masks = [half_mask(0, block), half_mask(1, block)]

    def pick(i, carry):
        out = pl.ds(pl.multiple_of(i * block, block), block)
        for j in range(heads):
            src = pl.ds(class_start(i, base + j, block), block)
            lanes = slice(j // 2 * 128, j // 2 * 128 + 128)
            doz_ref[j, out, :] = cls_ref[src, lanes] * masks[j % 2]
        return carry

    lax.fori_loop(0, CLASSES, pick, 0)
    unit = eye(2 * SLOT)
    for h in range(heads):
        turned = dot_nt(unit, doz_ref[h])[h % 2 * SLOT : h % 2 * SLOT + SLOT]
        delta_ref[h] = jnp.sum(turned * attn_t_ref[h], axis=0, keepdims=True)

    dqt_ref[...] = jnp.zeros_like(dqt_ref)
    copies = {}
    for level in range(levels):
        queries = max(half >> level, 128)
        keys = slice(level * half, level * half + half)
        transpose_heads(rk_ref, 0, level * half, half, kt_ref, heads)

        def remote(pair, carry):
            counts = pair_counts(half, queries, half, level)
            dk = jnp.zeros((half, 128), f32)
            dv = jnp.zeros((half, 128), f32)
            for side in range(2):
                h = 2 * pair + side
                q, do = qz_ref[h, :queries, :], doz_ref[h, :queries, :]
                p = jnp.exp2(dot_nt(rk_ref[pair, keys, :], q) - bound_ref[h, :, :queries]) * counts
                ds = p * (dot_nt(rk_ref[pairs + pair, keys, :], do) - delta_ref[h, :, :queries])
                p, ds = p.astype(bf16), ds.astype(bf16)
                dv = dv + dot(p, do)
                dk = dk + dot(ds, q)
                dqt_ref[h, :, :queries] += dot(kt_ref[h, :, :half], ds)
            sb_ref[pair, keys, :] = dk.astype(bf16)
            sb_ref[pairs + pair, keys, :] = dv.astype(bf16)
            return carry

        lax.fori_loop(0, pairs, remote, 0)
        for apart, offset, count in slots_of(level, half):
            copies[apart] = pltpu.make_async_remote_copy(
                src_ref=sb_ref.at[:, offset : offset + count, :],
                dst_ref=rg_ref.at[:, offset : offset + count, :],
                send_sem=send_sem.at[apart - 1],
                recv_sem=recv_sem.at[apart - 1],
                device_id={"seq": peer_of(me, apart)},
                device_id_type=MESH,
            )
            copies[apart].start()

    transpose_heads(kv_ref, 0, 0, rows, kt_ref, heads)

    def local(pair, carry):
        counts = pair_counts(half, half, half, None)
        for qt in range(2):
            there = slice(qt * half, qt * half + half)
            for side in range(2):
                h = 2 * pair + side
                q, do = qz_ref[h, there, :], doz_ref[h, there, :]
                for kt in range(2):
                    keys = slice(kt * half, kt * half + half)
                    p = jnp.exp2(dot_nt(kv_ref[pair, keys, :], q) - bound_ref[h, :, there])
                    if qt == 0 and kt == 0:
                        p = p * counts
                    ds = p * (dot_nt(kv_ref[pairs + pair, keys, :], do) - delta_ref[h, :, there])
                    p_ref[side, keys, :] = p.astype(bf16)
                    ds_ref[side, keys, :] = ds.astype(bf16)
                dv = dot(p_ref[side], do)
                dk = dot(ds_ref[side], q)
                if qt == 0 and side == 0:
                    dkv_ref[pairs + pair] = dv
                    dkv_ref[pair] = dk
                else:
                    dkv_ref[pairs + pair] += dv
                    dkv_ref[pair] += dk
                dqt_ref[h, :, there] += dot(kt_ref[h], ds_ref[side])
        return carry

    lax.fori_loop(0, pairs, local, 0)
    for pair in range(pairs):
        dq_ref[pair] = (
            jnp.concatenate([dqt_ref[2 * pair], dqt_ref[2 * pair + 1]], axis=0) * (1.0 / LOG2E)
        ).T
    for apart, offset, count in slots:
        copies[apart].wait_recv()
        for tile in range(heads):
            dkv_ref[tile, :count, :] += rg_ref[tile, offset : offset + count, :].astype(f32)
    for pair in range(pairs):
        dkv_ref[pair] = dkv_ref[pair] * FACTOR
    from_heads([(dq_ref, pair) for pair in range(pairs)], base, d_ref.at[0], block)
    from_heads([(dkv_ref.at[:pairs], pair) for pair in range(pairs)], base, d_ref.at[1], block)
    from_heads([(dkv_ref.at[pairs:], pair) for pair in range(pairs)], base, d_ref.at[2], block)
    unspread = unspreader(heads * HD)

    def natural(t, carry):
        here = pl.ds(pl.multiple_of(t * CHUNK, CHUNK), CHUNK)
        for c in range(3):
            rows_here = dot(swap, d_ref[c, here, :]).astype(bf16)
            dmixed_ref[c, here, :] = dot(rows_here, unspread).astype(bf16)
        return carry

    lax.fori_loop(0, rows // CHUNK, natural, 0)
    for apart, _, _ in slots:
        copies[apart].wait_send()


def shape(dims, dtype):
    return jax.ShapeDtypeStruct(dims, dtype)


def project(tokens, aux, gain, w_qkv, heads):
    rows, width = tokens.shape
    return pl.pallas_call(
        partial(project_kernel, heads),
        out_shape=(
            shape((rows, width), bf16),
            shape((heads, rows, 128), bf16),
            shape((heads, rows, 128), bf16),
        ),
        in_specs=[VMEM] * 4,
        out_specs=(VMEM,) * 3,
        scratch_shapes=[pltpu.VMEM((rows, 3 * heads * SLOT), bf16)],
        compiler_params=pltpu.CompilerParams(vmem_limit_bytes=LIMIT),
    )(tokens, aux, gain.reshape(1, -1), w_qkv)


def attend(qz, kv, levels):
    heads, rows, _ = kv.shape
    half = rows // 2
    peers = (1 << levels) - 1
    return pl.pallas_call(
        partial(attend_kernel, levels, heads),
        out_shape=(
            shape((rows, heads * HD), bf16),
            shape((heads, SLOT, rows), f32),
            shape((heads, 1, rows), f32),
            shape((heads, levels * half, 128), bf16),
        ),
        in_specs=[VMEM] * 2,
        out_specs=(VMEM,) * 4,
        scratch_shapes=[
            pltpu.VMEM((heads, SLOT, rows), bf16),
            pltpu.VMEM((2, rows, half), f32),
            pltpu.VMEM((2, rows, half), bf16),
            pltpu.VMEM((heads, SLOT, rows), f32),
            pltpu.VMEM((heads, 1, rows), f32),
            pltpu.VMEM((heads // 2, rows, 128), f32),
            pltpu.VMEM((rows, heads * SLOT), bf16),
            pltpu.SemaphoreType.DMA((peers,)),
            pltpu.SemaphoreType.DMA((peers,)),
        ],
        compiler_params=pltpu.CompilerParams(
            vmem_limit_bytes=LIMIT, collective_id=0, has_side_effects=True
        ),
    )(qz, kv)


def attend_back(qz, kv, rk, d_attn, attn_t, bound, levels):
    heads, rows, _ = kv.shape
    half = rows // 2
    peers = (1 << levels) - 1
    return pl.pallas_call(
        partial(attend_back_kernel, levels, heads),
        out_shape=shape((3, rows, heads * HD), bf16),
        in_specs=[VMEM] * 6,
        out_specs=VMEM,
        scratch_shapes=[
            pltpu.VMEM((rows, heads * SLOT), bf16),
            pltpu.VMEM((heads, rows, 128), bf16),
            pltpu.VMEM((heads, 1, rows), f32),
            pltpu.VMEM((heads, SLOT, rows), bf16),
            pltpu.VMEM((2, rows, half), bf16),
            pltpu.VMEM((2, rows, half), bf16),
            pltpu.VMEM((heads, rows, 128), f32),
            pltpu.VMEM((heads, SLOT, rows), f32),
            pltpu.VMEM((heads // 2, rows, 128), f32),
            pltpu.VMEM((heads, levels * half, 128), bf16),
            pltpu.VMEM((heads, levels * half, 128), bf16),
            pltpu.VMEM((3, rows, heads * SLOT), bf16),
            pltpu.SemaphoreType.DMA((peers,)),
            pltpu.SemaphoreType.DMA((peers,)),
        ],
        compiler_params=pltpu.CompilerParams(
            vmem_limit_bytes=LIMIT, collective_id=1, has_side_effects=True
        ),
    )(qz, kv, rk, d_attn, attn_t, bound)


def normalize(rows_in, gain):
    centre = rows_in - jnp.mean(rows_in, axis=-1, keepdims=True)
    spread = jnp.mean(centre * centre, axis=-1, keepdims=True)
    return centre * lax.rsqrt(spread + EPS) * gain


def mask_columns(slide_ids, valid, wide):
    lane = jnp.arange(2 * wide, dtype=jnp.int32)[None, :]
    kind = lane % SLOT - HD
    slide, real = slide_ids[:, None], valid[:, None]
    query = ((kind >= 0) & (kind < 8) & (kind != slide)) | ((kind == 8) & (real == 1))
    key = ((kind >= 0) & (kind < 8) & (kind == slide)) | ((kind == 8) & (real == 0))
    return jnp.where(
        lane < wide, jnp.where(query, NEG, 0.0), jnp.where(key, 1.0, 0.0)
    ).astype(bf16)


def body(tokens, slide_ids, valid, norm_one, w_qkv, w_out, norm_two, w_up, w_down, cotangent):
    heads = w_out.shape[0] // HD
    levels = level_count(lax.axis_size("seq"))
    first = tokens.astype(f32)
    aux = mask_columns(slide_ids, valid, heads * SLOT)
    normed_low, qz, kv = project(tokens, aux, norm_one, w_qkv, heads)
    attn_low, attn_t, bound, rk = attend(qz, kv, levels)
    attn_term = jnp.dot(attn_low, w_out, preferred_element_type=f32)
    middle = first + lax.psum(attn_term.astype(bf16), "head").astype(f32)
    second, pull_two = jax.vjp(normalize, middle, norm_two)
    second_low = second.astype(bf16)
    up_proj = jnp.dot(second_low, w_up, preferred_element_type=f32)
    hidden, pull_gelu = jax.vjp(partial(jax.nn.gelu, approximate=False), up_proj)
    hidden_low = hidden.astype(bf16)
    mlp_term = jnp.dot(hidden_low, w_down, preferred_element_type=f32)
    output = (middle + lax.psum(mlp_term.astype(bf16), "head").astype(f32)).astype(bf16)
    grad_down = jnp.einsum("tf,td->fd", hidden_low, cotangent, preferred_element_type=f32)
    d_hidden = jnp.einsum("td,fd->tf", cotangent, w_down, preferred_element_type=f32)
    d_up = pull_gelu(d_hidden)[0].astype(bf16)
    grad_up = jnp.einsum("td,tf->df", second_low, d_up, preferred_element_type=f32)
    d_second_term = jnp.einsum("tf,df->td", d_up, w_up, preferred_element_type=f32)
    d_second = lax.psum(d_second_term.astype(bf16), "head").astype(f32)
    d_middle_norm, grad_norm_two = pull_two(d_second)
    d_middle = cotangent.astype(f32) + d_middle_norm
    d_branch = d_middle.astype(bf16)
    grad_out = jnp.einsum("te,td->ed", attn_low, d_branch, preferred_element_type=f32)
    d_attn = jnp.einsum("td,ed->te", d_branch, w_out, preferred_element_type=f32).astype(bf16)
    early = lax.psum(tuple(g.astype(bf16) for g in (grad_out, grad_up, grad_down)), "seq")
    d_mixed = attend_back(qz, kv, rk, d_attn, attn_t, bound, levels)
    grad_qkv = jnp.einsum("td,cte->cde", normed_low, d_mixed, preferred_element_type=f32)
    d_normed_term = jnp.einsum("cte,cde->td", d_mixed, w_qkv, preferred_element_type=f32)
    d_normed = lax.psum(d_normed_term.astype(bf16), "head").astype(f32)
    pull_one = jax.vjp(normalize, first, norm_one)[1]
    d_first, grad_norm_one = pull_one(d_normed)
    input_grad = d_middle + d_first
    norms = lax.psum(jnp.stack([grad_norm_one, grad_norm_two]), "seq")
    late = lax.psum(grad_qkv.astype(bf16), "seq")
    return (
        output, input_grad, norms[0], late.astype(f32), early[0].astype(f32), norms[1],
        early[1].astype(f32), early[2].astype(f32),
    )


def solution(mesh):
    placed = (
        P("seq", None), P("seq"), P("seq"), P(), P(None, None, "head"), P("head", None), P(),
        P(None, "head"), P("head", None), P("seq", None),
    )
    return jax.shard_map(
        body,
        mesh=mesh,
        in_specs=placed,
        out_specs=(
            P("seq", None), P("seq", None), P(), P(None, None, "head"), P("head", None), P(),
            P(None, "head"), P("head", None),
        ),
        check_vma=False,
    )
```

```python
from functools import partial

import jax
import jax.numpy as jnp
from jax import lax
from jax.experimental import pallas as pl
from jax.experimental.pallas import tpu as pltpu
from jax.sharding import PartitionSpec as P

HD = 48
SLOT = 64
CLASSES = 16
CHUNK = CLASSES * 16
EPS = 1e-05
NEG = -(2.0**30)
LOG2E = 1.4426950408889634
FACTOR = HD ** (-0.5)
MESH = pl.DeviceIdType.MESH
f32 = jnp.float32
bf16 = jnp.bfloat16
NT = (((1,), (1,)), ((), ()))
VMEM = pl.BlockSpec(memory_space=pltpu.VMEM)
LIMIT = 60 * 1024 * 1024


def dot(a, b):
    return jnp.dot(a, b, preferred_element_type=f32)


def dot_tn(a, b):
    return lax.dot_general(a, b, (((0,), (0,)), ((), ())), preferred_element_type=f32)


def dot_nt(a, b):
    return lax.dot_general(a, b, NT, preferred_element_type=f32)


def iota(shape, dim):
    return lax.broadcasted_iota(jnp.int32, shape, dim)


def one_hot(cond):
    return jnp.where(cond, 1.0, 0.0).astype(bf16)


def digit_swap():
    row, col = iota((CHUNK, CHUNK), 0), iota((CHUNK, CHUNK), 1)
    return one_hot(col == 16 * (row % 16) + row // 16)


def spreader(width):
    row, col = iota((width, width // HD * SLOT), 0), iota((width, width // HD * SLOT), 1)
    return one_hot(col == SLOT * (row // HD) + row % HD)


def unspreader(width):
    row, col = iota((width // HD * SLOT, width), 0), iota((width // HD * SLOT, width), 1)
    return one_hot(row == SLOT * (col // HD) + col % HD)


def eye(size):
    return one_hot(iota((size, size), 0) == iota((size, size), 1))


def bit_reverse(i):
    return i % 2 * 8 + i // 2 % 2 * 4 + i // 4 % 2 * 2 + i // 8


def peer_of(me, apart):
    out = me
    for bit in range(apart.bit_length()):
        if apart >> bit & 1:
            out = out + (1 << bit) * (1 - 2 * (me // (1 << bit) % 2))
    return out


def level_count(n_seq):
    count = 0
    while count < 4 and 2 << count <= n_seq:
        count += 1
    return count


def slots_of(level, half):
    rows = half >> level
    return [
        (apart, level * half + (apart - (1 << level)) * rows, rows)
        for apart in range(1 << level, 2 << level)
    ]


def depth_of(index, half):
    total = jnp.zeros(index.shape, f32)
    for level in range(4):
        total = total + jnp.where(index < half >> level, 1.0, 0.0)
    return total


def pair_counts(keys, queries, half, level):
    period = half if level is None else half >> level
    key = depth_of(iota((keys, queries), 0) % period, half)
    query = depth_of(iota((keys, queries), 1), half)
    return jnp.minimum(key, query) + (1.0 if level is None else -1.0 * level)


def greet(peers):
    barrier = pltpu.get_barrier_semaphore()
    for axis, peer in peers:
        pl.semaphore_signal(barrier, inc=1, device_id={axis: peer}, device_id_type=MESH)
    pl.semaphore_wait(barrier, len(peers))


def seq_sum(me, src, out, buf, sem, slot, order):
    lo, size, offset, halved, sent = 0, src.shape[0], 0, [], []
    halvings = min(2, len(order) - 1)
    for step, bit in enumerate(order):
        mine = me // (1 << bit) % 2
        peer = peer_of(me, 1 << bit)
        if step < halvings:
            size = size // 2
            give = pl.multiple_of(lo + (1 - mine) * size, 16)
            halved.append((bit, mine, lo))
            lo = pl.multiple_of(lo + mine * size, 16)
        else:
            give = lo
        here = pl.ds(lo, size)
        landed = slice(offset, offset + size)
        copy = remote(src.at[pl.ds(give, size)], buf.at[landed], sem, (slot, step), "seq", peer)
        copy.start()
        yield
        copy.wait_recv()
        if step < halvings:
            sent.append(copy)
        elif step < len(order) - 1:
            copy.wait_send()
        else:
            sent.append(copy)
        value = (src[here].astype(f32) + buf[landed].astype(f32)).astype(bf16)
        if step < len(order) - 1:
            src[here] = value
        else:
            out[here] = value
        offset += size
    for step, (bit, mine, before) in enumerate(reversed(halved)):
        here = out.at[pl.ds(lo, size)]
        copy = remote(here, here, sem, (slot, len(order) + step), "seq", peer_of(me, 1 << bit))
        copy.start()
        yield
        copy.wait_recv()
        sent.append(copy)
        lo, size = before, size * 2
    for copy in sent:
        copy.wait_send()


def gain_sum(all_bits, mine, got, sem):
    sent = []
    for step, (axis, bit) in enumerate(all_bits):
        peer = peer_of(lax.axis_index(axis), 1 << bit)
        copy = remote(mine.at[step], got.at[step], sem, (step,), axis, peer)
        copy.start()
        yield
        copy.wait_recv()
        sent.append(copy)
        mine[step + 1] = mine[step] + got[step]
    for copy in sent:
        copy.wait_send()


def pump(*jobs):
    for job in jobs:
        next(job, None)


def remote(src, dst, sem, index, axis, peer):
    return pltpu.make_async_remote_copy(
        src_ref=src,
        dst_ref=dst,
        send_sem=sem.at[(0,) + index],
        recv_sem=sem.at[(1,) + index],
        device_id={axis: peer},
        device_id_type=MESH,
    )


class Place:
    def __init__(self):
        self.me = lax.axis_index("head")
        self.core, self.side = self.me % 2, self.me // 2
        self.partner = self.me + 1 - 2 * self.core
        self.across = self.me + 2 - 4 * self.side

    def peers(self):
        return [("head", self.partner), ("head", self.across)]


class HeadSum:
    def __init__(self, place, term, got, half, last, sem, slot):
        self.place, self.term, self.got, self.half, self.last = place, term, got, half, last
        self.sem, self.slot = sem, slot

    def near(self, s):
        src = self.term.at[s, 1 - self.place.core]
        return remote(src, self.got.at[s], self.sem, (self.slot, s), "head", self.place.partner)

    def far(self, s):
        return remote(
            self.half.at[s], self.last.at[s], self.sem, (self.slot + 1, s), "head", self.place.across
        )

    def start(self, s):
        self.near(s).start()

    def forward(self, s):
        self.near(s).wait_recv()
        core, other = self.place.core, 1 - self.place.side
        both = self.term[s, core, other].astype(f32) + self.got[s, other].astype(f32)
        self.half[s] = both.astype(bf16)
        self.far(s).start()

    def total(self, s):
        self.far(s).wait_recv()
        core, side = self.place.core, self.place.side
        both = self.term[s, core, side].astype(f32) + self.got[s, side].astype(f32)
        return both + self.last[s].astype(f32)

    def finish(self, s):
        self.near(s).wait_send()
        self.far(s).wait_send()


class HeadSpread:
    def __init__(self, place, at, sem, slot):
        self.place, self.at, self.sem, self.slot = place, at, sem, slot

    def copy(self, s, kind):
        place = self.place
        ref = self.at(place.core, 1 - place.side if kind == 2 else place.side, s)
        peer = place.across if kind == 0 else place.partner
        return remote(ref, ref, self.sem, (self.slot + kind, s), "head", peer)

    def start(self, s):
        self.copy(s, 0).start()
        self.copy(s, 1).start()

    def relay(self, s):
        self.copy(s, 0).wait_recv()
        self.copy(s, 2).start()

    def arrive(self, s):
        self.copy(s, 1).wait_recv()
        self.copy(s, 2).wait_recv()

    def finish(self, s):
        for kind in range(3):
            self.copy(s, kind).wait_send()


def half_mask(which, rows):
    lane = iota((rows, 2 * SLOT), 1)
    return one_hot(lane // SLOT == which)


def to_classes(value, t, cls_ref, lanes, block):
    for c in range(CLASSES):
        start = pl.multiple_of(c * block + t * 16, 16)
        cls_ref[pl.ds(start, 16), lanes] = value[16 * c : 16 * c + 16]


def class_start(i, head, block):
    return pl.multiple_of((bit_reverse(i) + head) % CLASSES * block, block)


def place_start(c, head, block):
    return pl.multiple_of(bit_reverse((c + CLASSES - head) % CLASSES) * block, block)


def from_heads(src_refs, base, dst_ref, block):
    low = iota((block, 2 * SLOT), 1) < SLOT

    def step(c, carry):
        for tile, (ref, pair) in enumerate(src_refs):
            left = ref[pair, pl.ds(place_start(c, base + 2 * pair, block), block), :]
            right = ref[pair, pl.ds(place_start(c, base + 2 * pair + 1, block), block), :]
            both = jnp.where(low, left, right).astype(bf16)
            for t in range(block // 16):
                start = pl.multiple_of(t * CHUNK + c * 16, 16)
                dst_ref[pl.ds(start, 16), tile * 128 : tile * 128 + 128] = both[16 * t : 16 * t + 16]
        return carry

    lax.fori_loop(0, CLASSES, step, 0)


def project_kernel(heads, tokens_ref, aux_ref, gain_ref, w_ref, normed_ref, qz_ref, kv_ref, cls_ref):
    rows = tokens_ref.shape[0]
    block = rows // CLASSES
    width = heads * HD
    wide = heads * SLOT
    swap = digit_swap()
    spread = spreader(width)
    ones = jnp.where(iota((CHUNK, wide), 1) % SLOT >= HD, 1.0, 0.0)

    def step(t, carry):
        here = pl.ds(pl.multiple_of(t * CHUNK, CHUNK), CHUNK)
        x = tokens_ref[here, :].astype(f32)
        centre = x - jnp.mean(x, axis=-1, keepdims=True)
        spread_of = jnp.mean(centre * centre, axis=-1, keepdims=True)
        normed = (centre * lax.rsqrt(spread_of + EPS) * gain_ref[...]).astype(bf16)
        normed_ref[here, :] = normed
        for c in range(3):
            y = dot_nt(normed, w_ref[c])
            if c == 1:
                y = y * (FACTOR * LOG2E)
            y = dot(y.astype(bf16), spread)
            if c < 2:
                y = y + aux_ref[here, c * wide : c * wide + wide].astype(f32)
            else:
                y = y + ones
            y = dot(swap, y.astype(bf16)).astype(bf16)
            to_classes(y, t, cls_ref, slice(c * wide, c * wide + wide), block)
        return carry

    lax.fori_loop(0, rows // CHUNK, step, 0)
    base = lax.axis_index("head") * heads
    masks = [half_mask(0, block), half_mask(1, block)]

    def pick(i, carry):
        out = pl.ds(pl.multiple_of(i * block, block), block)
        for j in range(heads):
            src = pl.ds(class_start(i, base + j, block), block)
            lanes = slice(j // 2 * 128, j // 2 * 128 + 128)
            qz_ref[j, out, :] = cls_ref[src, lanes] * masks[j % 2]
        for tile in range(heads):
            pair = tile % (heads // 2)
            lanes = slice(wide + tile * 128, wide + tile * 128 + 128)
            left = cls_ref[pl.ds(class_start(i, base + 2 * pair, block), block), lanes]
            right = cls_ref[pl.ds(class_start(i, base + 2 * pair + 1, block), block), lanes]
            kv_ref[tile, out, :] = left * masks[0] + right * masks[1]
        return carry

    lax.fori_loop(0, CLASSES, pick, 0)


def transpose_heads(ref, first, start, count, out_ref, heads):
    unit = eye(2 * SLOT)
    for pair in range(heads // 2):
        turned = dot_nt(unit, ref[first + pair, start : start + count, :]).astype(bf16)
        out_ref[2 * pair, :, :count] = turned[:SLOT]
        out_ref[2 * pair + 1, :, :count] = turned[SLOT:]


def attend_kernel(
    levels, heads, qz_ref, kv_ref, attn_ref, attn_t_ref, bound_ref, rk_ref,
    vt_ref, s_ref, p_ref, acc_ref, m_ref, a_ref, d_ref, send_sem, recv_sem,
):
    rows = kv_ref.shape[1]
    half = rows // 2
    block = rows // CLASSES
    me = lax.axis_index("seq")
    slots = [slot for level in range(levels) for slot in slots_of(level, half)]
    greet([("seq", peer_of(me, apart)) for apart, _, _ in slots])
    copies = {}
    for apart, offset, count in slots:
        copies[apart] = pltpu.make_async_remote_copy(
            src_ref=kv_ref.at[:, 0:count, :],
            dst_ref=rk_ref.at[:, offset : offset + count, :],
            send_sem=send_sem.at[apart - 1],
            recv_sem=recv_sem.at[apart - 1],
            device_id={"seq": peer_of(me, apart)},
            device_id_type=MESH,
        )
        copies[apart].start()
    transpose_heads(kv_ref, heads // 2, 0, rows, vt_ref, heads)

    def local(pair, carry):
        counts = pair_counts(half, half, half, None)
        for qt in range(2):
            there = slice(qt * half, qt * half + half)
            for side in range(2):
                h = 2 * pair + side
                s_ref[side] = dot_nt(kv_ref[pair], qz_ref[h, there, :])
                top = jnp.max(s_ref[side], axis=0, keepdims=True)
                low = jnp.exp2(s_ref[side, :half] - top)
                if qt == 0:
                    low = low * counts
                p_ref[side, :half] = low.astype(bf16)
                p_ref[side, half:] = jnp.exp2(s_ref[side, half:] - top).astype(bf16)
                acc_ref[h, :, there] = dot(vt_ref[h], p_ref[side])
                m_ref[h, :, there] = top
        return carry

    lax.fori_loop(0, heads // 2, local, 0)

    for level in range(levels):
        queries = max(half >> level, 128)
        for apart, _, _ in slots_of(level, half):
            copies[apart].wait_recv()
        keys = slice(level * half, level * half + half)
        transpose_heads(rk_ref, heads // 2, level * half, half, vt_ref, heads)

        def remote(pair, carry):
            counts = pair_counts(half, queries, half, level)
            for side in range(2):
                h = 2 * pair + side
                s = dot_nt(rk_ref[pair, keys, :], qz_ref[h, :queries, :])
                if half >> level < queries:
                    s = s + jnp.where(counts > 0.0, 0.0, NEG)
                old = m_ref[h, :, :queries]
                top = jnp.maximum(old, jnp.max(s, axis=0, keepdims=True))
                p = (jnp.exp2(s - top) * counts).astype(bf16)
                acc_ref[h, :, :queries] = acc_ref[h, :, :queries] * jnp.exp2(old - top) + dot(
                    vt_ref[h, :, :half], p
                )
                m_ref[h, :, :queries] = top
            return carry

        lax.fori_loop(0, heads // 2, remote, 0)

    for h in range(heads):
        total = acc_ref[h, HD : HD + 1, :]
        bound_ref[h] = m_ref[h] + jnp.log2(total)
        attn_t_ref[h] = acc_ref[h] * (1.0 / total)
    for pair in range(heads // 2):
        a_ref[pair] = jnp.concatenate([attn_t_ref[2 * pair], attn_t_ref[2 * pair + 1]], axis=0).T
    base = lax.axis_index("head") * heads
    from_heads([(a_ref, pair) for pair in range(heads // 2)], base, d_ref, block)
    swap = digit_swap()
    unspread = unspreader(heads * HD)
    for t in range(rows // CHUNK):
        here = slice(t * CHUNK, t * CHUNK + CHUNK)
        natural = dot(swap, d_ref[here, :]).astype(bf16)
        attn_ref[here, :] = dot(natural, unspread).astype(bf16)
    for apart, _, _ in slots:
        copies[apart].wait_send()


def unit_rows(rows_in):
    centre = rows_in - jnp.mean(rows_in, axis=-1, keepdims=True)
    spread = jnp.mean(centre * centre, axis=-1, keepdims=True)
    scale = lax.rsqrt(spread + EPS)
    return centre * scale, scale


def norm_back(grad, gain, unit, scale):
    n = grad * gain
    shift = jnp.mean(n, axis=-1, keepdims=True)
    along = jnp.mean(n * unit, axis=-1, keepdims=True)
    return scale * (n - shift - unit * along)


PARTS = 4


def middle_kernel(
    attn_ref, w_out_ref, tokens_ref, gain_ref, w_up_ref, w_down_ref, cot_ref,
    d_attn_ref, middle_ref, d_middle_ref, mlp_ref, grad_out_ref, grad_up_ref, grad_down_ref, gain_grad_ref,
    a_ref, hidden_ref, d_hidden_ref, d_up_ref, second_ref, branch_ref,
    term_ref, got_ref, half_ref, last_ref, back_ref, back_got_ref, back_half_ref, back_last_ref, sem,
):
    own, width = middle_ref.shape
    sub = own // PARTS
    chunk = 4 * sub
    units = w_up_ref.shape[1]
    tile = 256
    place = Place()
    greet(place.peers())
    gain = gain_ref[...]
    forth = HeadSum(place, term_ref, got_ref, half_ref, last_ref, sem, 0)
    back = HeadSum(place, back_ref, back_got_ref, back_half_ref, back_last_ref, sem, 2)
    seconds = HeadSpread(place, lambda core, side, s: second_ref.at[s, core, side], sem, 4)
    branches = HeadSpread(place, lambda core, side, s: branch_ref.at[s, core, side], sem, 7)

    def rows_of(s, k):
        return pl.ds(pl.multiple_of((2 * (k % 2) + k // 2) * own + s * sub, sub), sub)

    def mine_of(s):
        return pl.ds(pl.multiple_of(place.me * own + s * sub, sub), sub)

    def owned(s):
        return pl.ds(pl.multiple_of(s * sub, sub), sub)

    def chunk_of(s):
        return pl.ds(pl.multiple_of(s * chunk, chunk), chunk)

    def gather(ref, s):
        return jnp.concatenate([ref[rows_of(s, k), :] for k in range(4)], axis=0)

    def split(ref, s, value):
        for k in range(4):
            ref[s, k // 2, k % 2] = value[k * sub : k * sub + sub]

    def joined(ref, s):
        return jnp.concatenate([ref[s, k // 2, k % 2] for k in range(4)], axis=0)

    def each(step):
        def run(s, carry):
            step(s)
            return carry

        lax.fori_loop(0, PARTS, run, 0)

    def project_out(s):
        a = gather(attn_ref, s)
        a_ref[chunk_of(s), :] = a
        split(term_ref, s, dot(a, w_out_ref[...]).astype(bf16))
        forth.start(s)

    def hidden_back(s):
        d_hidden_ref[chunk_of(s), :] = dot_nt(gather(cot_ref, s), w_down_ref[...])

    def norm_rows(s):
        rows = tokens_ref[mine_of(s), :].astype(f32) + forth.total(s)
        middle_ref[owned(s), :] = rows
        unit, _ = unit_rows(rows)
        second_ref[s, place.core, place.side] = (unit * gain).astype(bf16)
        seconds.start(s)

    def feed(s):
        second = joined(second_ref, s)
        for j in range(0, units, tile):
            lanes = slice(j, j + tile)
            up = dot(second, w_up_ref[:, lanes])
            cdf = 0.5 + 0.5 * lax.erf(up * (0.5**0.5))
            hidden = (up * cdf).astype(bf16)
            slope = cdf + up * jnp.exp2(up * up * (-0.5 * LOG2E)) * 0.3989422804014327
            for k in range(4):
                hidden_ref[rows_of(s, k), lanes] = hidden[k * sub : k * sub + sub]
            d_up_ref[chunk_of(s), lanes] = (d_hidden_ref[chunk_of(s), lanes] * slope).astype(bf16)

    def feed_sums(s):
        split(back_ref, s, dot_nt(d_up_ref[chunk_of(s), :], w_up_ref[...]).astype(bf16))
        back.start(s)
        down = dot(gather(hidden_ref, s), w_down_ref[...]).astype(bf16)
        for k in range(4):
            mlp_ref[0, k // 2, k % 2, owned(s), :] = down[k * sub : k * sub + sub]

    def norm_rows_back(s):
        grad = back.total(s)
        unit, scale = unit_rows(middle_ref[owned(s), :])
        gain_grad_ref[...] += jnp.sum(grad * unit, axis=0, keepdims=True)
        d_middle = cot_ref[mine_of(s), :].astype(f32) + norm_back(grad, gain, unit, scale)
        d_middle_ref[owned(s), :] = d_middle
        branch_ref[s, place.core, place.side] = d_middle.astype(bf16)
        branches.start(s)

    def attn_back(s):
        branches.arrive(s)
        d_attn = dot_nt(joined(branch_ref, s), w_out_ref[...]).astype(bf16)
        for k in range(4):
            d_attn_ref[rows_of(s, k), :] = d_attn[k * sub : k * sub + sub]

    gain_grad_ref[...] = jnp.zeros_like(gain_grad_ref)
    each(project_out)
    each(hidden_back)
    each(forth.forward)
    each(norm_rows)
    each(seconds.relay)

    def tick(s, carry):
        seconds.arrive(s)
        feed(s)

        @pl.when(s >= 1)
        def _():
            back.forward(s - 1)

        @pl.when(s >= 2)
        def _():
            norm_rows_back(s - 2)

        @pl.when(s >= 3)
        def _():
            branches.relay(s - 3)

        feed_sums(s)
        return carry

    lax.fori_loop(0, PARTS, tick, 0)
    back.forward(PARTS - 1)
    norm_rows_back(PARTS - 2)
    for j in range(0, units, tile):
        grad_down_ref[j : j + tile, :] = dot_tn(hidden_ref[:, j : j + tile], cot_ref[...]).astype(bf16)
    branches.relay(PARTS - 3)
    norm_rows_back(PARTS - 1)
    for j in range(0, width, tile):
        second = second_ref[:, :, :, :, j : j + tile].reshape(PARTS * chunk, tile)
        grad_up_ref[j : j + tile, :] = dot_tn(second, d_up_ref[...]).astype(bf16)
    branches.relay(PARTS - 2)
    branches.relay(PARTS - 1)
    each(attn_back)
    for j in range(0, width, tile):
        branch = branch_ref[:, :, :, :, j : j + tile].reshape(PARTS * chunk, tile)
        grad_out_ref[:, j : j + tile] = dot_tn(a_ref[...], branch).astype(bf16)
    for mover in (forth, back, seconds, branches):
        each(mover.finish)


def back_kernel(
    levels, heads, orders,
    qz_ref, kv_ref, rk_ref, da_ref, attn_t_ref, bound_ref, middle_ref, d_middle_ref, mlp_ref,
    part_out_ref, part_up_ref, part_down_ref, part_gain_ref, tokens_ref, gain_ref, normed_ref, w_ref,
    output_ref, input_grad_ref, grad_out_ref, grad_up_ref, grad_down_ref, grad_qkv_ref, gains_ref,
    cls_ref, doz_ref, delta_ref, kt_ref, p_ref, ds_ref, dkv_ref, dqt_ref, dq_ref, sb_ref, rg_ref, d_ref,
    dm_ref, mlp_got_ref, mlp_half_ref, mlp_last_ref, term_ref, got_ref, half_ref, last_ref,
    src_out_ref, src_up_ref, src_down_ref, src_qkv_ref, buf_out_ref, buf_up_ref, buf_down_ref, buf_qkv_ref,
    gain_mine_ref, gain_got_ref, send_sem, recv_sem, head_sem, part_sem, seq_sem, gain_sem,
):
    rows = kv_ref.shape[1]
    half = rows // 2
    block = rows // CLASSES
    own = rows // 4
    sub = own // PARTS
    pairs = heads // 2
    wide = heads * SLOT
    width = heads * HD
    me = lax.axis_index("seq")
    base = lax.axis_index("head") * heads
    place = Place()
    slots = [slot for level in range(levels) for slot in slots_of(level, half)]
    apart_all = sorted({apart for apart, _, _ in slots} | {1 << bit for bit in orders[0]})
    greet([("seq", peer_of(me, apart)) for apart in apart_all] + place.peers())

    def mine_of(s, rows_each):
        return pl.ds(pl.multiple_of(place.me * own + s * rows_each, rows_each), rows_each)

    def natural_at(ref, rows_each):
        def at(core, side, s):
            start = (2 * side + core) * own + s * rows_each
            return ref.at[pl.ds(pl.multiple_of(start, rows_each), rows_each), :]

        return at

    mlp_sum = HeadSum(place, mlp_ref, mlp_got_ref, mlp_half_ref, mlp_last_ref, head_sem, 0)
    outputs = HeadSpread(place, natural_at(output_ref, own), head_sem, 2)
    normed_sum = HeadSum(place, term_ref, got_ref, half_ref, last_ref, part_sem, 0)
    inputs = HeadSpread(place, natural_at(input_grad_ref, sub), part_sem, 2)
    src_up_ref[...] = part_up_ref[...]
    src_down_ref[...] = part_down_ref[...]
    src_out_ref[...] = part_out_ref[...]
    ups = seq_sum(me, src_up_ref, grad_up_ref, buf_up_ref, seq_sem, 0, orders[0])
    downs = seq_sum(me, src_down_ref, grad_down_ref, buf_down_ref, seq_sem, 1, orders[1])
    outs = seq_sum(me, src_out_ref, grad_out_ref, buf_out_ref, seq_sem, 2, orders[0])
    mlp_sum.start(0)
    pump(ups, downs)

    swap = digit_swap()
    spread = spreader(width)
    for t in range(rows // CHUNK):
        y = dot(da_ref[t * CHUNK : t * CHUNK + CHUNK, :], spread).astype(bf16)
        y = dot(swap, y).astype(bf16)
        to_classes(y, t, cls_ref, slice(0, wide), block)
    masks = [half_mask(0, block), half_mask(1, block)]

    def pick(i, carry):
        out = pl.ds(pl.multiple_of(i * block, block), block)
        for j in range(heads):
            src = pl.ds(class_start(i, base + j, block), block)
            lanes = slice(j // 2 * 128, j // 2 * 128 + 128)
            doz_ref[j, out, :] = cls_ref[src, lanes] * masks[j % 2]
        return carry

    lax.fori_loop(0, CLASSES, pick, 0)
    unit = eye(2 * SLOT)
    for h in range(heads):
        turned = dot_nt(unit, doz_ref[h])[h % 2 * SLOT : h % 2 * SLOT + SLOT]
        delta_ref[h] = jnp.sum(turned * attn_t_ref[h], axis=0, keepdims=True)
    mlp_sum.forward(0)

    dqt_ref[...] = jnp.zeros_like(dqt_ref)
    copies = {}
    for level in range(levels):
        queries = max(half >> level, 128)
        keys = slice(level * half, level * half + half)
        transpose_heads(rk_ref, 0, level * half, half, kt_ref, heads)

        def remote_keys(pair, carry):
            counts = pair_counts(half, queries, half, level)
            dk = jnp.zeros((half, 128), f32)
            dv = jnp.zeros((half, 128), f32)
            for side in range(2):
                h = 2 * pair + side
                q, do = qz_ref[h, :queries, :], doz_ref[h, :queries, :]
                p = jnp.exp2(dot_nt(rk_ref[pair, keys, :], q) - bound_ref[h, :, :queries]) * counts
                ds = p * (dot_nt(rk_ref[pairs + pair, keys, :], do) - delta_ref[h, :, :queries])
                p, ds = p.astype(bf16), ds.astype(bf16)
                dv = dv + dot(p, do)
                dk = dk + dot(ds, q)
                dqt_ref[h, :, :queries] += dot(kt_ref[h, :, :half], ds)
            sb_ref[pair, keys, :] = dk.astype(bf16)
            sb_ref[pairs + pair, keys, :] = dv.astype(bf16)
            return carry

        lax.fori_loop(0, pairs, remote_keys, 0)
        for apart, offset, count in slots_of(level, half):
            copies[apart] = pltpu.make_async_remote_copy(
                src_ref=sb_ref.at[:, offset : offset + count, :],
                dst_ref=rg_ref.at[:, offset : offset + count, :],
                send_sem=send_sem.at[apart - 1],
                recv_sem=recv_sem.at[apart - 1],
                device_id={"seq": peer_of(me, apart)},
                device_id_type=MESH,
            )
            copies[apart].start()

    output_ref[mine_of(0, own), :] = (middle_ref[...] + mlp_sum.total(0)).astype(bf16)
    outputs.start(0)
    pump(ups, downs, outs)
    transpose_heads(kv_ref, 0, 0, rows, kt_ref, heads)

    def local(pair, carry):
        counts = pair_counts(half, half, half, None)
        for qt in range(2):
            there = slice(qt * half, qt * half + half)
            for side in range(2):
                h = 2 * pair + side
                q, do = qz_ref[h, there, :], doz_ref[h, there, :]
                for kt in range(2):
                    keys = slice(kt * half, kt * half + half)
                    p = jnp.exp2(dot_nt(kv_ref[pair, keys, :], q) - bound_ref[h, :, there])
                    if qt == 0 and kt == 0:
                        p = p * counts
                    ds = p * (dot_nt(kv_ref[pairs + pair, keys, :], do) - delta_ref[h, :, there])
                    p_ref[side, keys, :] = p.astype(bf16)
                    ds_ref[side, keys, :] = ds.astype(bf16)
                dv = dot(p_ref[side], do)
                dk = dot(ds_ref[side], q)
                if qt == 0 and side == 0:
                    dkv_ref[pairs + pair] = dv
                    dkv_ref[pair] = dk
                else:
                    dkv_ref[pairs + pair] += dv
                    dkv_ref[pair] += dk
                dqt_ref[h, :, there] += dot(kt_ref[h], ds_ref[side])
        return carry

    for pair in range(pairs):
        local(pair, 0)
        if pair == 0:
            outputs.relay(0)
        pump(ups, downs, outs)
    for pair in range(pairs):
        dq_ref[pair] = (
            jnp.concatenate([dqt_ref[2 * pair], dqt_ref[2 * pair + 1]], axis=0) * (1.0 / LOG2E)
        ).T
    for apart, offset, count in slots:
        copies[apart].wait_recv()
        for tile in range(heads):
            dkv_ref[tile, :count, :] += rg_ref[tile, offset : offset + count, :].astype(f32)
    for pair in range(pairs):
        dkv_ref[pair] = dkv_ref[pair] * FACTOR
    from_heads([(dq_ref, pair) for pair in range(pairs)], base, d_ref.at[0], block)
    from_heads([(dkv_ref.at[:pairs], pair) for pair in range(pairs)], base, d_ref.at[1], block)
    from_heads([(dkv_ref.at[pairs:], pair) for pair in range(pairs)], base, d_ref.at[2], block)
    unspread = unspreader(width)

    def natural(k, carry):
        core = (place.core + 1 + k // 2) % 2
        side = k % 2
        here = pl.ds(pl.multiple_of((2 * side + core) * CHUNK, CHUNK), CHUNK)
        term = jnp.zeros((CHUNK, normed_ref.shape[1]), f32)
        for c in range(3):
            rows_here = dot(swap, d_ref[c, here, :]).astype(bf16)
            mixed = dot(rows_here, unspread).astype(bf16)
            dm_ref[c, here, :] = mixed
            term = term + dot(mixed, w_ref[c])
        term = term.astype(bf16)
        for s in range(PARTS):
            term_ref[s, core, side] = term[s * sub : s * sub + sub]
        return carry

    def each(step):
        def run(s, carry):
            step(s)
            return carry

        lax.fori_loop(0, PARTS, run, 0)

    lax.fori_loop(0, 2, natural, 0)
    each(normed_sum.start)
    lax.fori_loop(2, 4, natural, 0)
    each(normed_sum.forward)
    for c in range(3):
        src_qkv_ref[c] = dot_tn(dm_ref[c], normed_ref[...]).astype(bf16)
    qkvs = [
        seq_sum(me, src_qkv_ref.at[c], grad_qkv_ref.at[c], buf_qkv_ref.at[c], seq_sem, 3 + c, orders[c % 2])
        for c in range(3)
    ]
    pump(*qkvs)
    gain = gain_ref[...]
    gain_mine_ref[0] = jnp.zeros_like(gain_mine_ref[0])
    gain_mine_ref[0, 1:2, :] = part_gain_ref[...]

    def rows_back(s):
        grad = normed_sum.total(s)
        unit_in, scale = unit_rows(tokens_ref[mine_of(s, sub), :].astype(f32))
        gain_mine_ref[0, 0:1, :] += jnp.sum(grad * unit_in, axis=0, keepdims=True)
        here = pl.ds(pl.multiple_of(s * sub, sub), sub)
        grad_in = d_middle_ref[here, :] + norm_back(grad, gain, unit_in, scale)
        input_grad_ref[mine_of(s, sub), :] = grad_in.astype(bf16)
        inputs.start(s)

    each(rows_back)
    bits = [("head", 0), ("head", 1)] + [("seq", bit) for bit in orders[0]]
    gains = gain_sum(bits, gain_mine_ref, gain_got_ref, gain_sem)
    pump(ups, downs, outs, gains, *qkvs)
    each(inputs.relay)
    for _ in range(2 * len(bits) + 4):
        pump(gains, ups, downs, outs, *qkvs)
    gains_ref[...] = gain_mine_ref[len(bits)]
    each(inputs.arrive)
    outputs.arrive(0)
    each(normed_sum.finish)
    each(inputs.finish)
    mlp_sum.finish(0)
    outputs.finish(0)
    for apart, _, _ in slots:
        copies[apart].wait_send()


def shape(dims, dtype):
    return jax.ShapeDtypeStruct(dims, dtype)


def project(tokens, aux, gain, w_qkv, heads):
    rows, width = tokens.shape
    return pl.pallas_call(
        partial(project_kernel, heads),
        out_shape=(
            shape((rows, width), bf16),
            shape((heads, rows, 128), bf16),
            shape((heads, rows, 128), bf16),
        ),
        in_specs=[VMEM] * 4,
        out_specs=(VMEM,) * 3,
        scratch_shapes=[pltpu.VMEM((rows, 3 * heads * SLOT), bf16)],
        compiler_params=pltpu.CompilerParams(vmem_limit_bytes=LIMIT),
    )(tokens, aux, gain.reshape(1, -1), w_qkv)


def attend(qz, kv, levels):
    heads, rows, _ = kv.shape
    half = rows // 2
    peers = (1 << levels) - 1
    return pl.pallas_call(
        partial(attend_kernel, levels, heads),
        out_shape=(
            shape((rows, heads * HD), bf16),
            shape((heads, SLOT, rows), f32),
            shape((heads, 1, rows), f32),
            shape((heads, levels * half, 128), bf16),
        ),
        in_specs=[VMEM] * 2,
        out_specs=(VMEM,) * 4,
        scratch_shapes=[
            pltpu.VMEM((heads, SLOT, rows), bf16),
            pltpu.VMEM((2, rows, half), f32),
            pltpu.VMEM((2, rows, half), bf16),
            pltpu.VMEM((heads, SLOT, rows), f32),
            pltpu.VMEM((heads, 1, rows), f32),
            pltpu.VMEM((heads // 2, rows, 128), f32),
            pltpu.VMEM((rows, heads * SLOT), bf16),
            pltpu.SemaphoreType.DMA((peers,)),
            pltpu.SemaphoreType.DMA((peers,)),
        ],
        compiler_params=pltpu.CompilerParams(
            vmem_limit_bytes=LIMIT, collective_id=0, has_side_effects=True
        ),
    )(qz, kv)


def middle(attn, w_out, tokens, gain, w_up, w_down, cotangent):
    rows, width = tokens.shape
    units = w_up.shape[1]
    own = rows // 4
    sub = own // PARTS
    parts = lambda *dims: pltpu.VMEM((PARTS,) + dims + (sub, width), bf16)
    return pl.pallas_call(
        middle_kernel,
        out_shape=(
            shape(attn.shape, bf16),
            shape((own, width), f32),
            shape((own, width), f32),
            shape((1, 2, 2, own, width), bf16),
            shape(w_out.shape, bf16),
            shape(w_up.shape, bf16),
            shape(w_down.shape, bf16),
            shape((1, width), f32),
        ),
        in_specs=[VMEM] * 7,
        out_specs=(VMEM,) * 8,
        scratch_shapes=[
            pltpu.VMEM(attn.shape, bf16),
            pltpu.VMEM((rows, units), bf16),
            pltpu.VMEM((rows, units), f32),
            pltpu.VMEM((rows, units), bf16),
            parts(2, 2), parts(2, 2),
            parts(2, 2), parts(2), parts(), parts(),
            parts(2, 2), parts(2), parts(), parts(),
            pltpu.SemaphoreType.DMA((2, 10, PARTS)),
        ],
        compiler_params=pltpu.CompilerParams(
            vmem_limit_bytes=LIMIT, collective_id=2, has_side_effects=True
        ),
    )(attn, w_out, tokens, gain.reshape(1, -1), w_up, w_down, cotangent)


def back(levels, bits, qz, kv, rk, d_attn, attn_t, bound, mid, gain, tokens, normed, w_qkv):
    middle_own, d_middle, mlp, part_out, part_up, part_down, part_gain = mid
    heads, rows, _ = kv.shape
    half = rows // 2
    own = rows // 4
    sub = own // PARTS
    width = tokens.shape[1]
    wide = heads * SLOT
    peers = (1 << levels) - 1
    orders = (list(range(bits)), [1, 0][:bits] + list(range(2, bits))) if bits > 1 else ([0], [0])
    halvings = min(2, bits - 1)

    def landing(dims):
        total, size = 0, dims[-2]
        for step in range(bits):
            size = size // 2 if step < halvings else size
            total += size
        return pltpu.VMEM(dims[:-2] + (total, dims[-1]), bf16)

    parts = lambda *dims: pltpu.VMEM((PARTS,) + dims + (sub, width), bf16)
    qkv_dims = w_qkv.shape
    return pl.pallas_call(
        partial(back_kernel, levels, heads, orders),
        out_shape=(
            shape((rows, width), bf16),
            shape((rows, width), bf16),
            shape(part_out.shape, bf16),
            shape(part_up.shape, bf16),
            shape(part_down.shape, bf16),
            shape(qkv_dims, bf16),
            shape((8, width), f32),
        ),
        in_specs=[VMEM] * 17,
        out_specs=(VMEM,) * 7,
        scratch_shapes=[
            pltpu.VMEM((rows, wide), bf16),
            pltpu.VMEM((heads, rows, 128), bf16),
            pltpu.VMEM((heads, 1, rows), f32),
            pltpu.VMEM((heads, SLOT, rows), bf16),
            pltpu.VMEM((2, rows, half), bf16),
            pltpu.VMEM((2, rows, half), bf16),
            pltpu.VMEM((heads, rows, 128), f32),
            pltpu.VMEM((heads, SLOT, rows), f32),
            pltpu.VMEM((heads // 2, rows, 128), f32),
            pltpu.VMEM((heads, levels * half, 128), bf16),
            pltpu.VMEM((heads, levels * half, 128), bf16),
            pltpu.VMEM((3, rows, wide), bf16),
            pltpu.VMEM((3, rows, heads * HD), bf16),
            pltpu.VMEM((1, 2, own, width), bf16),
            pltpu.VMEM((1, own, width), bf16),
            pltpu.VMEM((1, own, width), bf16),
            parts(2, 2), parts(2), parts(), parts(),
            pltpu.VMEM(part_out.shape, bf16),
            pltpu.VMEM(part_up.shape, bf16),
            pltpu.VMEM(part_down.shape, bf16),
            pltpu.VMEM(qkv_dims, bf16),
            landing(part_out.shape), landing(part_up.shape), landing(part_down.shape), landing(qkv_dims),
            pltpu.VMEM((bits + 3, 8, width), f32),
            pltpu.VMEM((bits + 2, 8, width), f32),
            pltpu.SemaphoreType.DMA((peers,)),
            pltpu.SemaphoreType.DMA((peers,)),
            pltpu.SemaphoreType.DMA((2, 5, 1)),
            pltpu.SemaphoreType.DMA((2, 5, PARTS)),
            pltpu.SemaphoreType.DMA((2, 6, bits + 2)),
            pltpu.SemaphoreType.DMA((2, bits + 2)),
        ],
        compiler_params=pltpu.CompilerParams(
            vmem_limit_bytes=LIMIT, collective_id=1, has_side_effects=True
        ),
    )(
        qz, kv, rk, d_attn, attn_t, bound, middle_own, d_middle, mlp, part_out, part_up, part_down,
        part_gain, tokens, gain.reshape(1, -1), normed, w_qkv,
    )


def mask_columns(slide_ids, valid, wide):
    lane = jnp.arange(2 * wide, dtype=jnp.int32)[None, :]
    kind = lane % SLOT - HD
    slide, real = slide_ids[:, None], valid[:, None]
    query = ((kind >= 0) & (kind < 8) & (kind != slide)) | ((kind == 8) & (real == 1))
    key = ((kind >= 0) & (kind < 8) & (kind == slide)) | ((kind == 8) & (real == 0))
    return jnp.where(
        lane < wide, jnp.where(query, NEG, 0.0), jnp.where(key, 1.0, 0.0)
    ).astype(bf16)


def body(tokens, slide_ids, valid, norm_one, w_qkv, w_out, norm_two, w_up, w_down, cotangent):
    heads = w_out.shape[0] // HD
    n_seq = lax.axis_size("seq")
    levels = level_count(n_seq)
    aux = mask_columns(slide_ids, valid, heads * SLOT)
    w_turned = jnp.swapaxes(w_qkv, 1, 2)
    normed, qz, kv = project(tokens, aux, norm_one, w_turned, heads)
    attn_low, attn_t, bound, rk = attend(qz, kv, levels)
    d_attn, *mid = middle(attn_low, w_out, tokens, norm_two, w_up, w_down, cotangent)
    output, input_grad, grad_out, grad_up, grad_down, grad_qkv, gains = back(
        levels, n_seq.bit_length() - 1, qz, kv, rk, d_attn, attn_t, bound, mid,
        norm_one, tokens, normed, w_turned,
    )
    return (
        output, input_grad.astype(f32), gains[0], jnp.swapaxes(grad_qkv, 1, 2).astype(f32),
        grad_out.astype(f32), gains[1], grad_up.astype(f32), grad_down.astype(f32),
    )


def solution(mesh):
    placed = (
        P("seq", None), P("seq"), P("seq"), P(), P(None, None, "head"), P("head", None), P(),
        P(None, "head"), P("head", None), P("seq", None),
    )
    return jax.shard_map(
        body,
        mesh=mesh,
        in_specs=placed,
        out_specs=(
            P("seq", None), P("seq", None), P(), P(None, None, "head"), P("head", None), P(),
            P(None, "head"), P("head", None),
        ),
        check_vma=False,
    )
```

```python
from functools import partial

import jax
import jax.numpy as jnp
from jax import lax
from jax.experimental import pallas as pl
from jax.experimental.pallas import tpu as pltpu
from jax.sharding import PartitionSpec as P

HD = 48
SLOT = 64
CLASSES = 16
CHUNK = CLASSES * 16
EPS = 1e-05
NEG = -(2.0**30)
LOG2E = 1.4426950408889634
FACTOR = HD ** (-0.5)
MESH = pl.DeviceIdType.MESH
f32 = jnp.float32
bf16 = jnp.bfloat16
NT = (((1,), (1,)), ((), ()))
VMEM = pl.BlockSpec(memory_space=pltpu.VMEM)
LIMIT = 60 * 1024 * 1024


def dot(a, b):
    return jnp.dot(a, b, preferred_element_type=f32)


def dot_tn(a, b):
    return lax.dot_general(a, b, (((0,), (0,)), ((), ())), preferred_element_type=f32)


def dot_nt(a, b):
    return lax.dot_general(a, b, NT, preferred_element_type=f32)


def iota(shape, dim):
    return lax.broadcasted_iota(jnp.int32, shape, dim)


def one_hot(cond):
    return jnp.where(cond, 1.0, 0.0).astype(bf16)


def digit_swap():
    row, col = iota((CHUNK, CHUNK), 0), iota((CHUNK, CHUNK), 1)
    return one_hot(col == 16 * (row % 16) + row // 16)


def spreader(width):
    row, col = iota((width, width // HD * SLOT), 0), iota((width, width // HD * SLOT), 1)
    return one_hot(col == SLOT * (row // HD) + row % HD)


def unspreader(width):
    row, col = iota((width // HD * SLOT, width), 0), iota((width // HD * SLOT, width), 1)
    return one_hot(row == SLOT * (col // HD) + col % HD)


def eye(size):
    return one_hot(iota((size, size), 0) == iota((size, size), 1))


def bit_reverse(i):
    return i % 2 * 8 + i // 2 % 2 * 4 + i // 4 % 2 * 2 + i // 8


def peer_of(me, apart):
    out = me
    for bit in range(apart.bit_length()):
        if apart >> bit & 1:
            out = out + (1 << bit) * (1 - 2 * (me // (1 << bit) % 2))
    return out


def level_count(n_seq):
    count = 0
    while count < 4 and 2 << count <= n_seq:
        count += 1
    return count


def slots_of(level, half):
    rows = half >> level
    return [
        (apart, level * half + (apart - (1 << level)) * rows, rows)
        for apart in range(1 << level, 2 << level)
    ]


def depth_of(index, half):
    total = jnp.zeros(index.shape, f32)
    for level in range(4):
        total = total + jnp.where(index < half >> level, 1.0, 0.0)
    return total


def pair_counts(keys, queries, half, level):
    period = half if level is None else half >> level
    key = depth_of(iota((keys, queries), 0) % period, half)
    query = depth_of(iota((keys, queries), 1), half)
    return jnp.minimum(key, query) + (1.0 if level is None else -1.0 * level)


def greet(peers):
    barrier = pltpu.get_barrier_semaphore()
    for axis, peer in peers:
        pl.semaphore_signal(barrier, inc=1, device_id={axis: peer}, device_id_type=MESH)
    pl.semaphore_wait(barrier, len(peers))


def seq_sum(me, src, out, buf, sem, slot, order, part=0, parts=1):
    size, offset = src.shape[0] // parts, buf.shape[0] // parts * part
    lo, halved, sent = size * part, [], []
    halvings = min(2, len(order) - 1)
    for step, bit in enumerate(order):
        mine = me // (1 << bit) % 2
        peer = peer_of(me, 1 << bit)
        if step < halvings:
            size = size // 2
            give = pl.multiple_of(lo + (1 - mine) * size, 16)
            halved.append((bit, mine, lo))
            lo = pl.multiple_of(lo + mine * size, 16)
        else:
            give = lo
        here = pl.ds(lo, size)
        landed = slice(offset, offset + size)
        copy = remote(src.at[pl.ds(give, size)], buf.at[landed], sem, (slot, step), "seq", peer)
        copy.start()
        yield
        copy.wait_recv()
        if step < halvings:
            sent.append(copy)
        elif step < len(order) - 1:
            copy.wait_send()
        else:
            sent.append(copy)
        value = (src[here].astype(f32) + buf[landed].astype(f32)).astype(bf16)
        if step < len(order) - 1:
            src[here] = value
        else:
            out[here] = value
        offset += size
    for step, (bit, mine, before) in enumerate(reversed(halved)):
        here = out.at[pl.ds(lo, size)]
        copy = remote(here, here, sem, (slot, len(order) + step), "seq", peer_of(me, 1 << bit))
        copy.start()
        yield
        copy.wait_recv()
        sent.append(copy)
        lo, size = before, size * 2
    for copy in sent:
        copy.wait_send()


def gain_sum(all_bits, mine, got, sem):
    sent = []
    for step, (axis, bit) in enumerate(all_bits):
        peer = peer_of(lax.axis_index(axis), 1 << bit)
        copy = remote(mine.at[step], got.at[step], sem, (step,), axis, peer)
        copy.start()
        yield
        copy.wait_recv()
        sent.append(copy)
        mine[step + 1] = mine[step] + got[step]
    for copy in sent:
        copy.wait_send()


def pump(*jobs):
    for job in jobs:
        next(job, None)


def remote(src, dst, sem, index, axis, peer):
    return pltpu.make_async_remote_copy(
        src_ref=src,
        dst_ref=dst,
        send_sem=sem.at[(0,) + index],
        recv_sem=sem.at[(1,) + index],
        device_id={axis: peer},
        device_id_type=MESH,
    )


class Place:
    def __init__(self):
        self.me = lax.axis_index("head")
        self.core, self.side = self.me % 2, self.me // 2
        self.partner = self.me + 1 - 2 * self.core
        self.across = self.me + 2 - 4 * self.side

    def peers(self):
        return [("head", self.partner), ("head", self.across)]


class HeadSum:
    def __init__(self, place, term, got, half, last, sem, slot):
        self.place, self.term, self.got, self.half, self.last = place, term, got, half, last
        self.sem, self.slot = sem, slot

    def near(self, s):
        src = self.term.at[s, 1 - self.place.core]
        return remote(src, self.got.at[s], self.sem, (self.slot, s), "head", self.place.partner)

    def far(self, s):
        return remote(
            self.half.at[s], self.last.at[s], self.sem, (self.slot + 1, s), "head", self.place.across
        )

    def start(self, s):
        self.near(s).start()

    def forward(self, s):
        self.near(s).wait_recv()
        core, other = self.place.core, 1 - self.place.side
        both = self.term[s, core, other].astype(f32) + self.got[s, other].astype(f32)
        self.half[s] = both.astype(bf16)
        self.far(s).start()

    def total(self, s):
        self.far(s).wait_recv()
        core, side = self.place.core, self.place.side
        both = self.term[s, core, side].astype(f32) + self.got[s, side].astype(f32)
        return both + self.last[s].astype(f32)

    def finish(self, s):
        self.near(s).wait_send()
        self.far(s).wait_send()


class HeadSpread:
    def __init__(self, place, at, sem, slot):
        self.place, self.at, self.sem, self.slot = place, at, sem, slot

    def copy(self, s, kind):
        place = self.place
        ref = self.at(place.core, 1 - place.side if kind == 2 else place.side, s)
        peer = place.across if kind == 0 else place.partner
        return remote(ref, ref, self.sem, (self.slot + kind, s), "head", peer)

    def start(self, s):
        self.copy(s, 0).start()
        self.copy(s, 1).start()

    def relay(self, s):
        self.copy(s, 0).wait_recv()
        self.copy(s, 2).start()

    def arrive(self, s):
        self.copy(s, 1).wait_recv()
        self.copy(s, 2).wait_recv()

    def finish(self, s):
        for kind in range(3):
            self.copy(s, kind).wait_send()


def half_mask(which, rows):
    lane = iota((rows, 2 * SLOT), 1)
    return one_hot(lane // SLOT == which)


def to_classes(value, t, cls_ref, lanes, block):
    for c in range(CLASSES):
        start = pl.multiple_of(c * block + t * 16, 16)
        cls_ref[pl.ds(start, 16), lanes] = value[16 * c : 16 * c + 16]


def class_start(i, head, block):
    return pl.multiple_of((bit_reverse(i) + head) % CLASSES * block, block)


def place_start(c, head, block):
    return pl.multiple_of(bit_reverse((c + CLASSES - head) % CLASSES) * block, block)


def from_heads(src_refs, base, dst_ref, block):
    low = iota((block, 2 * SLOT), 1) < SLOT

    def step(c, carry):
        for tile, (ref, pair) in enumerate(src_refs):
            left = ref[pair, pl.ds(place_start(c, base + 2 * pair, block), block), :]
            right = ref[pair, pl.ds(place_start(c, base + 2 * pair + 1, block), block), :]
            both = jnp.where(low, left, right).astype(bf16)
            for t in range(block // 16):
                start = pl.multiple_of(t * CHUNK + c * 16, 16)
                dst_ref[pl.ds(start, 16), tile * 128 : tile * 128 + 128] = both[16 * t : 16 * t + 16]
        return carry

    lax.fori_loop(0, CLASSES, step, 0)


def project_kernel(heads, tokens_ref, aux_ref, gain_ref, w_ref, normed_ref, qz_ref, kv_ref, cls_ref):
    rows = tokens_ref.shape[0]
    block = rows // CLASSES
    width = heads * HD
    wide = heads * SLOT
    swap = digit_swap()
    spread = spreader(width)
    ones = jnp.where(iota((CHUNK, wide), 1) % SLOT >= HD, 1.0, 0.0)

    def step(t, carry):
        here = pl.ds(pl.multiple_of(t * CHUNK, CHUNK), CHUNK)
        x = tokens_ref[here, :].astype(f32)
        centre = x - jnp.mean(x, axis=-1, keepdims=True)
        spread_of = jnp.mean(centre * centre, axis=-1, keepdims=True)
        normed = (centre * lax.rsqrt(spread_of + EPS) * gain_ref[...]).astype(bf16)
        normed_ref[here, :] = normed
        for c in range(3):
            y = dot_nt(normed, w_ref[c])
            if c == 1:
                y = y * (FACTOR * LOG2E)
            y = dot(y.astype(bf16), spread)
            if c < 2:
                y = y + aux_ref[here, c * wide : c * wide + wide].astype(f32)
            else:
                y = y + ones
            y = dot(swap, y.astype(bf16)).astype(bf16)
            to_classes(y, t, cls_ref, slice(c * wide, c * wide + wide), block)
        return carry

    lax.fori_loop(0, rows // CHUNK, step, 0)
    base = lax.axis_index("head") * heads
    masks = [half_mask(0, block), half_mask(1, block)]

    def pick(i, carry):
        out = pl.ds(pl.multiple_of(i * block, block), block)
        for j in range(heads):
            src = pl.ds(class_start(i, base + j, block), block)
            lanes = slice(j // 2 * 128, j // 2 * 128 + 128)
            qz_ref[j, out, :] = cls_ref[src, lanes] * masks[j % 2]
        for tile in range(heads):
            pair = tile % (heads // 2)
            lanes = slice(wide + tile * 128, wide + tile * 128 + 128)
            left = cls_ref[pl.ds(class_start(i, base + 2 * pair, block), block), lanes]
            right = cls_ref[pl.ds(class_start(i, base + 2 * pair + 1, block), block), lanes]
            kv_ref[tile, out, :] = left * masks[0] + right * masks[1]
        return carry

    lax.fori_loop(0, CLASSES, pick, 0)


def transpose_heads(ref, first, start, count, out_ref, heads):
    unit = eye(2 * SLOT)
    for pair in range(heads // 2):
        turned = dot_nt(unit, ref[first + pair, start : start + count, :]).astype(bf16)
        out_ref[2 * pair, :, :count] = turned[:SLOT]
        out_ref[2 * pair + 1, :, :count] = turned[SLOT:]


def attend_kernel(
    levels, heads, qz_ref, kv_ref, attn_ref, attn_t_ref, bound_ref, rk_ref,
    vt_ref, s_ref, p_ref, acc_ref, m_ref, a_ref, d_ref, send_sem, recv_sem,
):
    rows = kv_ref.shape[1]
    half = rows // 2
    block = rows // CLASSES
    me = lax.axis_index("seq")
    slots = [slot for level in range(levels) for slot in slots_of(level, half)]
    greet([("seq", peer_of(me, apart)) for apart, _, _ in slots])
    copies = {}
    for apart, offset, count in slots:
        copies[apart] = pltpu.make_async_remote_copy(
            src_ref=kv_ref.at[:, 0:count, :],
            dst_ref=rk_ref.at[:, offset : offset + count, :],
            send_sem=send_sem.at[apart - 1],
            recv_sem=recv_sem.at[apart - 1],
            device_id={"seq": peer_of(me, apart)},
            device_id_type=MESH,
        )
        copies[apart].start()
    transpose_heads(kv_ref, heads // 2, 0, rows, vt_ref, heads)

    def local(pair, carry):
        counts = pair_counts(half, half, half, None)
        for qt in range(2):
            there = slice(qt * half, qt * half + half)
            for side in range(2):
                h = 2 * pair + side
                s_ref[side] = dot_nt(kv_ref[pair], qz_ref[h, there, :])
                top = jnp.max(s_ref[side], axis=0, keepdims=True)
                low = jnp.exp2(s_ref[side, :half] - top)
                if qt == 0:
                    low = low * counts
                p_ref[side, :half] = low.astype(bf16)
                p_ref[side, half:] = jnp.exp2(s_ref[side, half:] - top).astype(bf16)
                acc_ref[h, :, there] = dot(vt_ref[h], p_ref[side])
                m_ref[h, :, there] = top
        return carry

    lax.fori_loop(0, heads // 2, local, 0)

    for level in range(levels):
        queries = max(half >> level, 128)
        for apart, _, _ in slots_of(level, half):
            copies[apart].wait_recv()
        keys = slice(level * half, level * half + half)
        transpose_heads(rk_ref, heads // 2, level * half, half, vt_ref, heads)

        def remote(pair, carry):
            counts = pair_counts(half, queries, half, level)
            for side in range(2):
                h = 2 * pair + side
                s = dot_nt(rk_ref[pair, keys, :], qz_ref[h, :queries, :])
                if half >> level < queries:
                    s = s + jnp.where(counts > 0.0, 0.0, NEG)
                old = m_ref[h, :, :queries]
                top = jnp.maximum(old, jnp.max(s, axis=0, keepdims=True))
                p = (jnp.exp2(s - top) * counts).astype(bf16)
                acc_ref[h, :, :queries] = acc_ref[h, :, :queries] * jnp.exp2(old - top) + dot(
                    vt_ref[h, :, :half], p
                )
                m_ref[h, :, :queries] = top
            return carry

        lax.fori_loop(0, heads // 2, remote, 0)

    for h in range(heads):
        total = acc_ref[h, HD : HD + 1, :]
        bound_ref[h] = m_ref[h] + jnp.log2(total)
        attn_t_ref[h] = acc_ref[h] * (1.0 / total)
    for pair in range(heads // 2):
        a_ref[pair] = jnp.concatenate([attn_t_ref[2 * pair], attn_t_ref[2 * pair + 1]], axis=0).T
    base = lax.axis_index("head") * heads
    from_heads([(a_ref, pair) for pair in range(heads // 2)], base, d_ref, block)
    swap = digit_swap()
    unspread = unspreader(heads * HD)
    for t in range(rows // CHUNK):
        here = slice(t * CHUNK, t * CHUNK + CHUNK)
        natural = dot(swap, d_ref[here, :]).astype(bf16)
        attn_ref[here, :] = dot(natural, unspread).astype(bf16)
    for apart, _, _ in slots:
        copies[apart].wait_send()


def unit_rows(rows_in):
    centre = rows_in - jnp.mean(rows_in, axis=-1, keepdims=True)
    spread = jnp.mean(centre * centre, axis=-1, keepdims=True)
    scale = lax.rsqrt(spread + EPS)
    return centre * scale, scale


def norm_back(grad, gain, unit, scale):
    n = grad * gain
    shift = jnp.mean(n, axis=-1, keepdims=True)
    along = jnp.mean(n * unit, axis=-1, keepdims=True)
    return scale * (n - shift - unit * along)


PARTS = 4


def middle_kernel(
    attn_ref, w_out_ref, tokens_ref, gain_ref, w_up_ref, w_down_ref, cot_ref,
    d_attn_ref, middle_ref, d_middle_ref, mlp_ref, grad_out_ref, grad_up_ref, grad_down_ref, gain_grad_ref,
    a_ref, hidden_ref, d_hidden_ref, d_up_ref, second_ref, branch_ref,
    term_ref, got_ref, half_ref, last_ref, back_ref, back_got_ref, back_half_ref, back_last_ref, sem,
):
    own, width = middle_ref.shape
    sub = own // PARTS
    chunk = 4 * sub
    units = w_up_ref.shape[1]
    tile = 256
    place = Place()
    greet(place.peers())
    gain = gain_ref[...]
    forth = HeadSum(place, term_ref, got_ref, half_ref, last_ref, sem, 0)
    back = HeadSum(place, back_ref, back_got_ref, back_half_ref, back_last_ref, sem, 2)
    seconds = HeadSpread(place, lambda core, side, s: second_ref.at[s, core, side], sem, 4)
    branches = HeadSpread(place, lambda core, side, s: branch_ref.at[s, core, side], sem, 7)

    def rows_of(s, k):
        return pl.ds(pl.multiple_of((2 * (k % 2) + k // 2) * own + s * sub, sub), sub)

    def mine_of(s):
        return pl.ds(pl.multiple_of(place.me * own + s * sub, sub), sub)

    def owned(s):
        return pl.ds(pl.multiple_of(s * sub, sub), sub)

    def chunk_of(s):
        return pl.ds(pl.multiple_of(s * chunk, chunk), chunk)

    def gather(ref, s):
        return jnp.concatenate([ref[rows_of(s, k), :] for k in range(4)], axis=0)

    def split(ref, s, value):
        for k in range(4):
            ref[s, k // 2, k % 2] = value[k * sub : k * sub + sub]

    def joined(ref, s):
        return jnp.concatenate([ref[s, k // 2, k % 2] for k in range(4)], axis=0)

    def each(step):
        def run(s, carry):
            step(s)
            return carry

        lax.fori_loop(0, PARTS, run, 0)

    def project_out(s):
        a = gather(attn_ref, s)
        a_ref[chunk_of(s), :] = a
        split(term_ref, s, dot(a, w_out_ref[...]).astype(bf16))
        forth.start(s)

    def hidden_back(s):
        d_hidden_ref[chunk_of(s), :] = dot_nt(gather(cot_ref, s), w_down_ref[...])

    def norm_rows(s):
        rows = tokens_ref[mine_of(s), :].astype(f32) + forth.total(s)
        middle_ref[owned(s), :] = rows
        unit, _ = unit_rows(rows)
        second_ref[s, place.core, place.side] = (unit * gain).astype(bf16)
        seconds.start(s)

    def feed(s):
        second = joined(second_ref, s)
        for j in range(0, units, tile):
            lanes = slice(j, j + tile)
            up = dot(second, w_up_ref[:, lanes])
            cdf = 0.5 + 0.5 * lax.erf(up * (0.5**0.5))
            hidden = (up * cdf).astype(bf16)
            slope = cdf + up * jnp.exp2(up * up * (-0.5 * LOG2E)) * 0.3989422804014327
            for k in range(4):
                hidden_ref[rows_of(s, k), lanes] = hidden[k * sub : k * sub + sub]
            d_up_ref[chunk_of(s), lanes] = (d_hidden_ref[chunk_of(s), lanes] * slope).astype(bf16)

    def feed_sums(s):
        split(back_ref, s, dot_nt(d_up_ref[chunk_of(s), :], w_up_ref[...]).astype(bf16))
        back.start(s)
        down = dot(gather(hidden_ref, s), w_down_ref[...]).astype(bf16)
        for k in range(4):
            mlp_ref[0, k // 2, k % 2, owned(s), :] = down[k * sub : k * sub + sub]

    def norm_rows_back(s):
        grad = back.total(s)
        unit, scale = unit_rows(middle_ref[owned(s), :])
        gain_grad_ref[...] += jnp.sum(grad * unit, axis=0, keepdims=True)
        d_middle = cot_ref[mine_of(s), :].astype(f32) + norm_back(grad, gain, unit, scale)
        d_middle_ref[owned(s), :] = d_middle
        branch_ref[s, place.core, place.side] = d_middle.astype(bf16)
        branches.start(s)

    def attn_back(s):
        branches.arrive(s)
        d_attn = dot_nt(joined(branch_ref, s), w_out_ref[...]).astype(bf16)
        for k in range(4):
            d_attn_ref[rows_of(s, k), :] = d_attn[k * sub : k * sub + sub]

    gain_grad_ref[...] = jnp.zeros_like(gain_grad_ref)
    each(project_out)
    each(hidden_back)
    each(forth.forward)
    each(norm_rows)
    each(seconds.relay)

    def tick(s, carry):
        seconds.arrive(s)
        feed(s)

        @pl.when(s >= 1)
        def _():
            back.forward(s - 1)

        @pl.when(s >= 2)
        def _():
            norm_rows_back(s - 2)

        @pl.when(s >= 3)
        def _():
            branches.relay(s - 3)

        feed_sums(s)
        return carry

    lax.fori_loop(0, PARTS, tick, 0)
    back.forward(PARTS - 1)
    norm_rows_back(PARTS - 2)
    for j in range(0, units, tile):
        grad_down_ref[j : j + tile, :] = dot_tn(hidden_ref[:, j : j + tile], cot_ref[...]).astype(bf16)
    branches.relay(PARTS - 3)
    norm_rows_back(PARTS - 1)
    for j in range(0, width, tile):
        second = second_ref[:, :, :, :, j : j + tile].reshape(PARTS * chunk, tile)
        grad_up_ref[j : j + tile, :] = dot_tn(second, d_up_ref[...]).astype(bf16)
    branches.relay(PARTS - 2)
    branches.relay(PARTS - 1)
    each(attn_back)
    for j in range(0, width, tile):
        branch = branch_ref[:, :, :, :, j : j + tile].reshape(PARTS * chunk, tile)
        grad_out_ref[:, j : j + tile] = dot_tn(a_ref[...], branch).astype(bf16)
    for mover in (forth, back, seconds, branches):
        each(mover.finish)


def back_kernel(
    levels, heads, orders,
    qz_ref, kv_ref, rk_ref, da_ref, attn_t_ref, bound_ref, middle_ref, d_middle_ref, mlp_ref,
    part_out_ref, part_up_ref, part_down_ref, part_gain_ref, tokens_ref, gain_ref, normed_ref, w_ref,
    output_ref, input_grad_ref, grad_out_ref, grad_up_ref, grad_down_ref, grad_qkv_ref, gains_ref,
    cls_ref, doz_ref, delta_ref, kt_ref, p_ref, ds_ref, dkv_ref, dqt_ref, dq_ref, sb_ref, rg_ref, d_ref,
    dm_ref, mlp_got_ref, mlp_half_ref, mlp_last_ref, term_ref, got_ref, half_ref, last_ref,
    src_out_ref, src_up_ref, src_down_ref, src_qkv_ref, buf_out_ref, buf_up_ref, buf_down_ref, buf_qkv_ref,
    gain_mine_ref, gain_got_ref, send_sem, recv_sem, head_sem, part_sem, seq_sem, gain_sem,
):
    rows = kv_ref.shape[1]
    half = rows // 2
    block = rows // CLASSES
    own = rows // 4
    sub = own // PARTS
    pairs = heads // 2
    wide = heads * SLOT
    width = heads * HD
    me = lax.axis_index("seq")
    base = lax.axis_index("head") * heads
    place = Place()
    slots = [slot for level in range(levels) for slot in slots_of(level, half)]
    apart_all = sorted({apart for apart, _, _ in slots} | {1 << bit for bit in orders[0]})
    greet([("seq", peer_of(me, apart)) for apart in apart_all] + place.peers())

    def mine_of(s, rows_each):
        return pl.ds(pl.multiple_of(place.me * own + s * rows_each, rows_each), rows_each)

    def natural_at(ref, rows_each):
        def at(core, side, s):
            start = (2 * side + core) * own + s * rows_each
            return ref.at[pl.ds(pl.multiple_of(start, rows_each), rows_each), :]

        return at

    mlp_sum = HeadSum(place, mlp_ref, mlp_got_ref, mlp_half_ref, mlp_last_ref, head_sem, 0)
    outputs = HeadSpread(place, natural_at(output_ref, own), head_sem, 2)
    normed_sum = HeadSum(place, term_ref, got_ref, half_ref, last_ref, part_sem, 0)
    inputs = HeadSpread(place, natural_at(input_grad_ref, sub), part_sem, 2)
    src_up_ref[...] = part_up_ref[...]
    src_down_ref[...] = part_down_ref[...]
    src_out_ref[...] = part_out_ref[...]
    u0, u1 = [
        seq_sum(me, src_up_ref, grad_up_ref, buf_up_ref, seq_sem, k, orders[0], k, 2) for k in range(2)
    ]
    d0, d1 = [
        seq_sum(me, src_down_ref, grad_down_ref, buf_down_ref, seq_sem, 2 + k, orders[k], k, 2)
        for k in range(2)
    ]
    outs = seq_sum(me, src_out_ref, grad_out_ref, buf_out_ref, seq_sem, 4, orders[0])
    mlp_sum.start(0)
    pump(u0, d1, u1, d0, outs)

    swap = digit_swap()
    spread = spreader(width)
    for t in range(rows // CHUNK):
        y = dot(da_ref[t * CHUNK : t * CHUNK + CHUNK, :], spread).astype(bf16)
        y = dot(swap, y).astype(bf16)
        to_classes(y, t, cls_ref, slice(0, wide), block)
    masks = [half_mask(0, block), half_mask(1, block)]

    def pick(i, carry):
        out = pl.ds(pl.multiple_of(i * block, block), block)
        for j in range(heads):
            src = pl.ds(class_start(i, base + j, block), block)
            lanes = slice(j // 2 * 128, j // 2 * 128 + 128)
            doz_ref[j, out, :] = cls_ref[src, lanes] * masks[j % 2]
        return carry

    lax.fori_loop(0, CLASSES, pick, 0)
    unit = eye(2 * SLOT)
    for h in range(heads):
        turned = dot_nt(unit, doz_ref[h])[h % 2 * SLOT : h % 2 * SLOT + SLOT]
        delta_ref[h] = jnp.sum(turned * attn_t_ref[h], axis=0, keepdims=True)
    mlp_sum.forward(0)
    pump(u0, d1)

    dqt_ref[...] = jnp.zeros_like(dqt_ref)
    copies = {}
    for level in range(levels):
        queries = max(half >> level, 128)
        keys = slice(level * half, level * half + half)
        transpose_heads(rk_ref, 0, level * half, half, kt_ref, heads)

        def remote_keys(pair, carry):
            counts = pair_counts(half, queries, half, level)
            dk = jnp.zeros((half, 128), f32)
            dv = jnp.zeros((half, 128), f32)
            for side in range(2):
                h = 2 * pair + side
                q, do = qz_ref[h, :queries, :], doz_ref[h, :queries, :]
                p = jnp.exp2(dot_nt(rk_ref[pair, keys, :], q) - bound_ref[h, :, :queries]) * counts
                ds = p * (dot_nt(rk_ref[pairs + pair, keys, :], do) - delta_ref[h, :, :queries])
                p, ds = p.astype(bf16), ds.astype(bf16)
                dv = dv + dot(p, do)
                dk = dk + dot(ds, q)
                dqt_ref[h, :, :queries] += dot(kt_ref[h, :, :half], ds)
            sb_ref[pair, keys, :] = dk.astype(bf16)
            sb_ref[pairs + pair, keys, :] = dv.astype(bf16)
            return carry

        lax.fori_loop(0, pairs, remote_keys, 0)
        for apart, offset, count in slots_of(level, half):
            copies[apart] = pltpu.make_async_remote_copy(
                src_ref=sb_ref.at[:, offset : offset + count, :],
                dst_ref=rg_ref.at[:, offset : offset + count, :],
                send_sem=send_sem.at[apart - 1],
                recv_sem=recv_sem.at[apart - 1],
                device_id={"seq": peer_of(me, apart)},
                device_id_type=MESH,
            )
            copies[apart].start()
        if level == 0:
            pump(u0, u1)

    output_ref[mine_of(0, own), :] = (middle_ref[...] + mlp_sum.total(0)).astype(bf16)
    outputs.start(0)
    pump(u1, d0)
    transpose_heads(kv_ref, 0, 0, rows, kt_ref, heads)

    def local(pair, qt):
        counts = pair_counts(half, half, half, None)
        there = slice(qt * half, qt * half + half)
        for side in range(2):
            h = 2 * pair + side
            q, do = qz_ref[h, there, :], doz_ref[h, there, :]
            for kt in range(2):
                keys = slice(kt * half, kt * half + half)
                p = jnp.exp2(dot_nt(kv_ref[pair, keys, :], q) - bound_ref[h, :, there])
                if qt == 0 and kt == 0:
                    p = p * counts
                ds = p * (dot_nt(kv_ref[pairs + pair, keys, :], do) - delta_ref[h, :, there])
                p_ref[side, keys, :] = p.astype(bf16)
                ds_ref[side, keys, :] = ds.astype(bf16)
            dv = dot(p_ref[side], do)
            dk = dot(ds_ref[side], q)
            if qt == 0 and side == 0:
                dkv_ref[pairs + pair] = dv
                dkv_ref[pair] = dk
            else:
                dkv_ref[pairs + pair] += dv
                dkv_ref[pair] += dk
            dqt_ref[h, :, there] += dot(kt_ref[h], ds_ref[side])

    turns = [(u0, outs, d1), (u1, d0), (u0, d1), (u1, d0, outs)]
    for turn in range(2 * pairs):
        local(turn // 2, turn % 2)
        if turn == 1:
            outputs.relay(0)
        pump(*turns[turn % 4])
    for pair in range(pairs):
        dq_ref[pair] = (
            jnp.concatenate([dqt_ref[2 * pair], dqt_ref[2 * pair + 1]], axis=0) * (1.0 / LOG2E)
        ).T
    for apart, offset, count in slots:
        copies[apart].wait_recv()
        for tile in range(heads):
            dkv_ref[tile, :count, :] += rg_ref[tile, offset : offset + count, :].astype(f32)
    for pair in range(pairs):
        dkv_ref[pair] = dkv_ref[pair] * FACTOR
    from_heads([(dq_ref, pair) for pair in range(pairs)], base, d_ref.at[0], block)
    pump(outs, d1)
    from_heads([(dkv_ref.at[:pairs], pair) for pair in range(pairs)], base, d_ref.at[1], block)
    from_heads([(dkv_ref.at[pairs:], pair) for pair in range(pairs)], base, d_ref.at[2], block)
    pump(d0, outs)
    unspread = unspreader(width)

    def natural(k, carry):
        core = (place.core + 1 + k // 2) % 2
        side = k % 2
        here = pl.ds(pl.multiple_of((2 * side + core) * CHUNK, CHUNK), CHUNK)
        term = jnp.zeros((CHUNK, normed_ref.shape[1]), f32)
        for c in range(3):
            rows_here = dot(swap, d_ref[c, here, :]).astype(bf16)
            mixed = dot(rows_here, unspread).astype(bf16)
            dm_ref[c, here, :] = mixed
            term = term + dot(mixed, w_ref[c])
        term = term.astype(bf16)
        for s in range(PARTS):
            term_ref[s, core, side] = term[s * sub : s * sub + sub]
        return carry

    def each(step):
        def run(s, carry):
            step(s)
            return carry

        lax.fori_loop(0, PARTS, run, 0)

    lax.fori_loop(0, 2, natural, 0)
    each(normed_sum.start)
    lax.fori_loop(2, 4, natural, 0)
    each(normed_sum.forward)
    for c in range(3):
        src_qkv_ref[c] = dot_tn(dm_ref[c], normed_ref[...]).astype(bf16)
    qkvs = [
        seq_sum(me, src_qkv_ref.at[c], grad_qkv_ref.at[c], buf_qkv_ref.at[c], seq_sem, 5 + c, orders[c % 2])
        for c in range(3)
    ]
    pump(*qkvs)
    gain = gain_ref[...]
    gain_mine_ref[0] = jnp.zeros_like(gain_mine_ref[0])
    gain_mine_ref[0, 1:2, :] = part_gain_ref[...]

    def rows_back(s):
        grad = normed_sum.total(s)
        unit_in, scale = unit_rows(tokens_ref[mine_of(s, sub), :].astype(f32))
        gain_mine_ref[0, 0:1, :] += jnp.sum(grad * unit_in, axis=0, keepdims=True)
        here = pl.ds(pl.multiple_of(s * sub, sub), sub)
        grad_in = d_middle_ref[here, :] + norm_back(grad, gain, unit_in, scale)
        input_grad_ref[mine_of(s, sub), :] = grad_in.astype(bf16)
        inputs.start(s)

    each(rows_back)
    bits = [("head", 0), ("head", 1)] + [("seq", bit) for bit in orders[0]]
    gains = gain_sum(bits, gain_mine_ref, gain_got_ref, gain_sem)
    pump(gains)
    for s in range(PARTS):
        pump(*qkvs, gains)
        inputs.relay(s)
    for _ in range(2 * len(bits) + 4):
        pump(gains, u0, u1, d1, d0, outs, *qkvs)
    gains_ref[...] = gain_mine_ref[len(bits)]
    each(inputs.arrive)
    outputs.arrive(0)
    each(normed_sum.finish)
    each(inputs.finish)
    mlp_sum.finish(0)
    outputs.finish(0)
    for apart, _, _ in slots:
        copies[apart].wait_send()


def shape(dims, dtype):
    return jax.ShapeDtypeStruct(dims, dtype)


def project(tokens, aux, gain, w_qkv, heads):
    rows, width = tokens.shape
    return pl.pallas_call(
        partial(project_kernel, heads),
        out_shape=(
            shape((rows, width), bf16),
            shape((heads, rows, 128), bf16),
            shape((heads, rows, 128), bf16),
        ),
        in_specs=[VMEM] * 4,
        out_specs=(VMEM,) * 3,
        scratch_shapes=[pltpu.VMEM((rows, 3 * heads * SLOT), bf16)],
        compiler_params=pltpu.CompilerParams(vmem_limit_bytes=LIMIT),
    )(tokens, aux, gain.reshape(1, -1), w_qkv)


def attend(qz, kv, levels):
    heads, rows, _ = kv.shape
    half = rows // 2
    peers = (1 << levels) - 1
    return pl.pallas_call(
        partial(attend_kernel, levels, heads),
        out_shape=(
            shape((rows, heads * HD), bf16),
            shape((heads, SLOT, rows), f32),
            shape((heads, 1, rows), f32),
            shape((heads, levels * half, 128), bf16),
        ),
        in_specs=[VMEM] * 2,
        out_specs=(VMEM,) * 4,
        scratch_shapes=[
            pltpu.VMEM((heads, SLOT, rows), bf16),
            pltpu.VMEM((2, rows, half), f32),
            pltpu.VMEM((2, rows, half), bf16),
            pltpu.VMEM((heads, SLOT, rows), f32),
            pltpu.VMEM((heads, 1, rows), f32),
            pltpu.VMEM((heads // 2, rows, 128), f32),
            pltpu.VMEM((rows, heads * SLOT), bf16),
            pltpu.SemaphoreType.DMA((peers,)),
            pltpu.SemaphoreType.DMA((peers,)),
        ],
        compiler_params=pltpu.CompilerParams(
            vmem_limit_bytes=LIMIT, collective_id=0, has_side_effects=True
        ),
    )(qz, kv)


def middle(attn, w_out, tokens, gain, w_up, w_down, cotangent):
    rows, width = tokens.shape
    units = w_up.shape[1]
    own = rows // 4
    sub = own // PARTS
    parts = lambda *dims: pltpu.VMEM((PARTS,) + dims + (sub, width), bf16)
    return pl.pallas_call(
        middle_kernel,
        out_shape=(
            shape(attn.shape, bf16),
            shape((own, width), f32),
            shape((own, width), f32),
            shape((1, 2, 2, own, width), bf16),
            shape(w_out.shape, bf16),
            shape(w_up.shape, bf16),
            shape(w_down.shape, bf16),
            shape((1, width), f32),
        ),
        in_specs=[VMEM] * 7,
        out_specs=(VMEM,) * 8,
        scratch_shapes=[
            pltpu.VMEM(attn.shape, bf16),
            pltpu.VMEM((rows, units), bf16),
            pltpu.VMEM((rows, units), f32),
            pltpu.VMEM((rows, units), bf16),
            parts(2, 2), parts(2, 2),
            parts(2, 2), parts(2), parts(), parts(),
            parts(2, 2), parts(2), parts(), parts(),
            pltpu.SemaphoreType.DMA((2, 10, PARTS)),
        ],
        compiler_params=pltpu.CompilerParams(
            vmem_limit_bytes=LIMIT, collective_id=2, has_side_effects=True
        ),
    )(attn, w_out, tokens, gain.reshape(1, -1), w_up, w_down, cotangent)


def back(levels, bits, qz, kv, rk, d_attn, attn_t, bound, mid, gain, tokens, normed, w_qkv):
    middle_own, d_middle, mlp, part_out, part_up, part_down, part_gain = mid
    heads, rows, _ = kv.shape
    half = rows // 2
    own = rows // 4
    sub = own // PARTS
    width = tokens.shape[1]
    wide = heads * SLOT
    peers = (1 << levels) - 1
    orders = (list(range(bits)), [1, 0][:bits] + list(range(2, bits))) if bits > 1 else ([0], [0])
    halvings = min(2, bits - 1)

    def landing(dims):
        total, size = 0, dims[-2]
        for step in range(bits):
            size = size // 2 if step < halvings else size
            total += size
        return pltpu.VMEM(dims[:-2] + (total, dims[-1]), bf16)

    parts = lambda *dims: pltpu.VMEM((PARTS,) + dims + (sub, width), bf16)
    qkv_dims = w_qkv.shape
    return pl.pallas_call(
        partial(back_kernel, levels, heads, orders),
        out_shape=(
            shape((rows, width), bf16),
            shape((rows, width), bf16),
            shape(part_out.shape, bf16),
            shape(part_up.shape, bf16),
            shape(part_down.shape, bf16),
            shape(qkv_dims, bf16),
            shape((8, width), f32),
        ),
        in_specs=[VMEM] * 17,
        out_specs=(VMEM,) * 7,
        scratch_shapes=[
            pltpu.VMEM((rows, wide), bf16),
            pltpu.VMEM((heads, rows, 128), bf16),
            pltpu.VMEM((heads, 1, rows), f32),
            pltpu.VMEM((heads, SLOT, rows), bf16),
            pltpu.VMEM((2, rows, half), bf16),
            pltpu.VMEM((2, rows, half), bf16),
            pltpu.VMEM((heads, rows, 128), f32),
            pltpu.VMEM((heads, SLOT, rows), f32),
            pltpu.VMEM((heads // 2, rows, 128), f32),
            pltpu.VMEM((heads, levels * half, 128), bf16),
            pltpu.VMEM((heads, levels * half, 128), bf16),
            pltpu.VMEM((3, rows, wide), bf16),
            pltpu.VMEM((3, rows, heads * HD), bf16),
            pltpu.VMEM((1, 2, own, width), bf16),
            pltpu.VMEM((1, own, width), bf16),
            pltpu.VMEM((1, own, width), bf16),
            parts(2, 2), parts(2), parts(), parts(),
            pltpu.VMEM(part_out.shape, bf16),
            pltpu.VMEM(part_up.shape, bf16),
            pltpu.VMEM(part_down.shape, bf16),
            pltpu.VMEM(qkv_dims, bf16),
            landing(part_out.shape), landing(part_up.shape), landing(part_down.shape), landing(qkv_dims),
            pltpu.VMEM((bits + 3, 8, width), f32),
            pltpu.VMEM((bits + 2, 8, width), f32),
            pltpu.SemaphoreType.DMA((peers,)),
            pltpu.SemaphoreType.DMA((peers,)),
            pltpu.SemaphoreType.DMA((2, 5, 1)),
            pltpu.SemaphoreType.DMA((2, 5, PARTS)),
            pltpu.SemaphoreType.DMA((2, 8, bits + 2)),
            pltpu.SemaphoreType.DMA((2, bits + 2)),
        ],
        compiler_params=pltpu.CompilerParams(
            vmem_limit_bytes=LIMIT, collective_id=1, has_side_effects=True
        ),
    )(
        qz, kv, rk, d_attn, attn_t, bound, middle_own, d_middle, mlp, part_out, part_up, part_down,
        part_gain, tokens, gain.reshape(1, -1), normed, w_qkv,
    )


def mask_columns(slide_ids, valid, wide):
    lane = jnp.arange(2 * wide, dtype=jnp.int32)[None, :]
    kind = lane % SLOT - HD
    slide, real = slide_ids[:, None], valid[:, None]
    query = ((kind >= 0) & (kind < 8) & (kind != slide)) | ((kind == 8) & (real == 1))
    key = ((kind >= 0) & (kind < 8) & (kind == slide)) | ((kind == 8) & (real == 0))
    return jnp.where(
        lane < wide, jnp.where(query, NEG, 0.0), jnp.where(key, 1.0, 0.0)
    ).astype(bf16)


def body(tokens, slide_ids, valid, norm_one, w_qkv, w_out, norm_two, w_up, w_down, cotangent):
    heads = w_out.shape[0] // HD
    n_seq = lax.axis_size("seq")
    levels = level_count(n_seq)
    aux = mask_columns(slide_ids, valid, heads * SLOT)
    w_turned = jnp.swapaxes(w_qkv, 1, 2)
    normed, qz, kv = project(tokens, aux, norm_one, w_turned, heads)
    attn_low, attn_t, bound, rk = attend(qz, kv, levels)
    d_attn, *mid = middle(attn_low, w_out, tokens, norm_two, w_up, w_down, cotangent)
    output, input_grad, grad_out, grad_up, grad_down, grad_qkv, gains = back(
        levels, n_seq.bit_length() - 1, qz, kv, rk, d_attn, attn_t, bound, mid,
        norm_one, tokens, normed, w_turned,
    )
    return (
        output, input_grad.astype(f32), gains[0], jnp.swapaxes(grad_qkv, 1, 2).astype(f32),
        grad_out.astype(f32), gains[1], grad_up.astype(f32), grad_down.astype(f32),
    )


def solution(mesh):
    placed = (
        P("seq", None), P("seq"), P("seq"), P(), P(None, None, "head"), P("head", None), P(),
        P(None, "head"), P("head", None), P("seq", None),
    )
    return jax.shard_map(
        body,
        mesh=mesh,
        in_specs=placed,
        out_specs=(
            P("seq", None), P("seq", None), P(), P(None, None, "head"), P("head", None), P(),
            P(None, "head"), P("head", None),
        ),
        check_vma=False,
    )
```
